32 devices in a mesh: groups: 2 (over y), seq: 4 (over z), strand: 2 (over core), chan: 2 (over x).
Axes of the slice: x: 2, y: 2, z: 4, core: 2. Of those that a mesh axis runs over, the one named last changes fastest.
Arguments:
- seq_in: bfloat16 [2, 6144, 512], P('strand', ('groups', 'seq', 'chan')), parts along dimension 1, may hold values from -6 to 6
- conv_norm: float32 [2, 512], replicated, may hold values from 0.1 to 1.9
- conv_weight: bfloat16 [2, 3, 512, 512], P(None, None, None, ('seq', 'chan')), may hold values from -0.15625 to 0.15625
- ff_norm: float32 [2, 512], replicated, may hold values from 0.1 to 1.9
- up_weight: bfloat16 [2, 512, 2048], P(None, None, ('seq', 'chan')), may hold values from -0.25 to 0.25
- down_weight: bfloat16 [2, 2048, 512], P(None, ('seq', 'chan')), may hold values from -0.125 to 0.125
- head_norm: float32 [512], replicated, may hold values from 0.1 to 1.9
- value_weight: bfloat16 [512, 512], replicated, may hold values from -0.25 to 0.25
- gate_weight: bfloat16 [512, 512], replicated, may hold values from -0.25 to 0.25
- out_weight: bfloat16 [512, 512], replicated, may hold values from -0.25 to 0.25
Outputs:
- strand_out: bfloat16 [2, 6144, 512], P('strand', ('groups', 'seq', 'chan')), parts along dimension 1
The draws below stay inside these ranges and needn't reach their ends.
There are 2 independent parts, one for each index of `groups`. The reference program is written for one: setup_inputs(seed, part) draws one part's arguments, and reference() takes and returns one part's arrays. A program takes and returns all parts, laid end to end along the dimension named above; an argument that names none is the same for every part. Nothing has to cross between parts.
All inputs are finite; a program needn't handle non-finite values.
Results may differ from the reference program's by a relative error of at most 0.015.
Values may be sent and summed in bfloat16 or wider, within the bound.
No kernel may reach another device: no remote copies, remote signals or barrier semaphores. Data moves between devices by JAX's collectives and lax.ppermute only.
A program may use at most 64 MiB of HBM per device.

```python
import jax
import jax.numpy as jnp
from jax import lax

D = 512
FF = 2048
POS_DEV = 384
BLOCKS = 2
POSITIONS = 3072
N_SEQ = 4
N_CHAN = 2


def shard_levels(key, shape, pieces, smallest, largest):
    level, own = 1.0, jax.random.fold_in(key, 6)
    for position, parts in pieces:
        draws = jnp.exp(jax.random.uniform(jax.random.fold_in(own, position), (parts,), jnp.float32, smallest / len(pieces), largest / len(pieces)))
        level = level * jnp.repeat(draws, shape[position] // parts).reshape([-1 if axis == position else 1 for axis in range(len(shape))])
    return level


def noise(rng, shape, width, most, split=(), kind=jnp.bfloat16):
    level = shard_levels(rng, shape, split, -0.22, 0.18) if split else 1.0
    array = jax.random.normal(rng, shape, jnp.float32) * width * level
    return jnp.minimum(jnp.maximum(array, -most), most).astype(kind)


def setup_inputs(seed: int = 0, part: int = 0) -> dict:
    seeds = jax.random.split(jax.random.key(seed), 11)
    part_splits = jax.random.split(jax.random.fold_in(seeds[10], part), 11)
    return {
        "seq_in": noise(part_splits[0], (2, POSITIONS, D), 1.0, 6.0, ((0, 2), (1, 8))),
        "conv_norm": jnp.clip(1.0 + 0.18 * jax.random.normal(seeds[1], (BLOCKS, D), jnp.float32), 0.1, 1.9),
        "conv_weight": noise(seeds[2], (BLOCKS, 3, D, D), (3 * D) ** -0.5, 0.15625, ((3, 8),)),
        "ff_norm": jnp.clip(1.0 + 0.18 * jax.random.normal(seeds[3], (BLOCKS, D), jnp.float32), 0.1, 1.9),
        "up_weight": noise(seeds[4], (BLOCKS, D, FF), D ** -0.5, 0.25, ((2, 8),)),
        "down_weight": noise(seeds[5], (BLOCKS, FF, D), FF ** -0.5, 0.125, ((1, 8),)),
        "head_norm": jnp.clip(1.0 + 0.18 * jax.random.normal(seeds[6], (D,), jnp.float32), 0.1, 1.9),
        "value_weight": noise(seeds[7], (D, D), D ** -0.5, 0.25),
        "gate_weight": noise(seeds[8], (D, D), D ** -0.5, 0.25),
        "out_weight": noise(seeds[9], (D, D), D ** -0.5, 0.25),
    }


def normalize(values, gain):
    return values * jax.lax.rsqrt(lax.optimization_barrier(jnp.mean(values * values, axis=-1, keepdims=True)) + 1e-06) * gain

def rowdot(left, right):
    flat = left.reshape(-1, left.shape[-1])
    result = jnp.dot(flat, right, preferred_element_type=jnp.float32)
    return result.reshape(left.shape[:-1] + (right.shape[-1],))

def reference(seq_in, conv_norm, conv_weight, ff_norm, up_weight, down_weight, head_norm, value_weight, gate_weight, out_weight):
    state = seq_in.astype(jnp.float32)
    length = state.shape[1]
    for block in range(BLOCKS):
        dilation = POS_DEV * N_CHAN * min(2 ** block, N_SEQ // 2)
        normed = normalize(state, conv_norm[block]).astype(jnp.bfloat16)
        before = jnp.pad(normed, ((0, 0), (dilation, 0), (0, 0)))[:, :length]
        after = jnp.pad(normed, ((0, 0), (0, dilation), (0, 0)))[:, dilation:]
        conv = rowdot(before, conv_weight[block, 0]) + rowdot(normed, conv_weight[block, 1]) + rowdot(after, conv_weight[block, 2])
        state = state + conv.astype(jnp.bfloat16).astype(jnp.float32)
        mixed = normalize(state, ff_norm[block]).astype(jnp.bfloat16)
        hidden = jax.nn.gelu(rowdot(mixed, up_weight[block])).astype(jnp.bfloat16)
        state = state + rowdot(hidden, down_weight[block])
    final = normalize(state, head_norm).astype(jnp.bfloat16)
    value = rowdot(final, value_weight)
    logits = rowdot(final, gate_weight).astype(jnp.bfloat16)
    mirrored = logits[::-1, ::-1]
    gated = (value * jax.nn.sigmoid(mirrored.astype(jnp.float32))).astype(jnp.bfloat16)
    return rowdot(gated, out_weight).astype(jnp.bfloat16)
```

```python
import functools
import itertools

import jax
import jax.numpy as jnp
from jax import lax
from jax.experimental import pallas as pl
from jax.experimental.pallas import tpu as pltpu
from jax.sharding import PartitionSpec as P

AXES = ("groups", "seq", "strand", "chan")
BF16, F32 = jnp.bfloat16, jnp.float32
PARAMS = pltpu.CompilerParams(vmem_limit_bytes=40 * 2**20)
VMEM_SPEC = pl.BlockSpec(memory_space=pltpu.VMEM)
ANY_SPEC = pl.BlockSpec(memory_space=pl.ANY)


def normalize(values, gain):
    return values * lax.rsqrt(jnp.mean(values * values, axis=-1, keepdims=True) + 1e-06) * gain


def matmul(left, right):
    return jnp.dot(left, right, preferred_element_type=F32)


def matmul_nt(left, right):
    return lax.dot_general(left, right, (((1,), (1,)), ((), ())), preferred_element_type=F32)


def passed_along(value, axis, steps):
    count = lax.axis_size(axis)
    initial, last = (max(0, -steps), min(count, count - steps))
    return lax.ppermute(value, axis, [(source, source + steps) for source in range(initial, last)])


def swapped(x, axis, stride):
    return lax.ppermute(x, axis, [(i, i ^ 1 << stride) for i in range(lax.axis_size(axis))])


def local_plain(
    seq_in, conv_norm, conv_weight, ff_norm, up_weight, down_weight,
    head_norm, value_weight, gate_weight, out_weight,
):
    state = seq_in[0].astype(F32)
    seq_count = lax.axis_size("seq")
    for block in range(conv_weight.shape[0]):
        reach = min(2**block, seq_count // 2)
        normed = normalize(state, conv_norm[block]).astype(BF16)
        before = passed_along(normed, "seq", reach)
        after = passed_along(normed, "seq", -reach)
        piece = lax.all_gather(conv_weight[block], ("seq", "chan"), axis=2, tiled=True)
        total = matmul(before, piece[0]) + matmul(normed, piece[1]) + matmul(after, piece[2])
        state = state + total.astype(BF16).astype(F32)
        mixed = normalize(state, ff_norm[block]).astype(BF16)
        up = lax.all_gather(up_weight[block], ("seq", "chan"), axis=1, tiled=True)
        hidden = jax.nn.gelu(matmul(mixed, up)).astype(BF16)
        down = lax.all_gather(down_weight[block], ("seq", "chan"), axis=0, tiled=True)
        state = state + matmul(hidden, down)
    final = normalize(state, head_norm).astype(BF16)
    value = matmul(final, value_weight)
    bit_count = (seq_count * lax.axis_size("chan")).bit_length() - 1
    opposite = swapped(final, "strand", 0)
    for digit in range(bit_count):
        opposite = swapped(opposite, ("seq", "chan"), digit)
    opposite = jnp.flip(opposite, 0)
    mirrored = matmul(opposite, gate_weight).astype(BF16)
    gated = (value * jax.nn.sigmoid(mirrored.astype(F32))).astype(BF16)
    return matmul(gated, out_weight).astype(BF16)[None]


def moved(value, go):
    sizes = [lax.axis_size(a) for a in AXES]

    def flat(at):
        number = 0
        for n, k in zip(sizes, at):
            number = number * n + k
        return number

    pairs = [(flat(at), flat(go(*at))) for at in itertools.product(*map(range, sizes))]
    return lax.ppermute(value, AXES, pairs)


def plan(count, block):
    def first(g):
        flip = (g + block) % 2
        return 1 + flip

    return first, count - 1


def origins(block, half_of_mine):
    g, i, c = (lax.axis_index(a) for a in ("groups", "seq", "chan"))
    n, m = lax.axis_size("seq"), lax.axis_size("chan")
    mine = 1 + lax.rem(g + block, 2)
    other = 1 + lax.rem(g + block + 1, 2)
    last = n - 1
    back = lambda k: lax.rem(i + n - k, n)
    x = 1 - c
    at = [
        (i, c), (back(mine), c), (back(last), c), (i, x),
        (back(mine), x), (back(last), x), (back(other), c), (back(other), x),
    ]
    return [a * m + b for a, b in at]


def gathered(mine, block):
    n = lax.axis_size("seq")
    first, last = plan(n, block)
    along = lambda v, k: moved(v, lambda g, i, s, c: (g, (i + k(g)) % n, s, c))
    across = lambda v: moved(v, lambda g, i, s, c: (g, i, s, 1 - c))
    planes = lambda v: moved(v, lambda g, i, s, c: (1 - g, i, s, c))
    a1 = along(mine, first)
    a2 = along(mine, lambda g: last)
    a3 = across(mine)
    a4 = across(a1)
    a5 = across(a2)
    a6 = planes(a1)
    a7 = planes(a4)
    return [a1, a2, a3, a4, a5, a6, a7]


def other_core(value):
    return moved(value, lambda g, i, s, c: (g, i, 1 - s, c))


def pack_kernel(conv_ref, up_ref, down_ref, mine_ref, other_ref):
    first = lax.axis_index("strand") == 0
    at = 0

    def put(whole):
        nonlocal at
        half = whole.shape[0] // 2
        top, low = whole[:half], whole[half:]
        mine_ref[at : at + half] = jnp.where(first, top, low)
        other_ref[at : at + half] = jnp.where(first, low, top)
        at += half

    put(up_ref[0].T)
    put(down_ref[0])
    for tap in range(conv_ref.shape[1]):
        put(conv_ref[0, tap].T)


def pack(conv_weight, up_weight, down_weight, block):
    taps, width, chans = conv_weight.shape[1:]
    hidden = up_weight.shape[2]
    rows = hidden + taps * chans // 2
    shape = jax.ShapeDtypeStruct((rows, width), BF16)
    index = lambda rank: (lambda i: (block,) + (0,) * (rank - 1))
    spec = lambda a: pl.BlockSpec((1,) + a.shape[1:], index(a.ndim))
    return pl.pallas_call(
        pack_kernel,
        out_shape=[shape, shape],
        grid=(1,),
        in_specs=[spec(conv_weight), spec(up_weight), spec(down_weight)],
        out_specs=[pl.BlockSpec((rows, width), lambda i: (0, 0))] * 2,
        compiler_params=PARAMS,
        name=f"pack{block}",
    )(conv_weight, up_weight, down_weight)


def split_kernel(rows_ref, *out_refs):
    n = lax.axis_size("seq")
    i, s = lax.axis_index("seq"), lax.axis_index("strand")
    size = out_refs[0].shape[0]
    for k, out in enumerate(out_refs):
        j = lax.rem(i + k, n)
        sub = jnp.where(s == 0, j, n - 1 - j)
        out[...] = rows_ref[pl.ds(pl.multiple_of(sub * size, size), size)]


def join_kernel(*refs):
    *parts, out = refs
    n = lax.axis_size("seq")
    i, s = lax.axis_index("seq"), lax.axis_index("strand")
    size = parts[0].shape[0]
    for k, part in enumerate(parts):
        j = lax.rem(i + n - k, n)
        sub = jnp.where(s == 0, j, n - 1 - j)
        out[pl.ds(pl.multiple_of(sub * size, size), size)] = part[...]


def conv_kernel(block, parts, hidden, gain_ref, *refs):
    n = lax.axis_size("seq")
    states, refs = refs[:parts], refs[parts:]
    count = (len(refs) - 4) // 2
    mine, other = refs[:count], refs[count : 2 * count]
    out, weight, acc, sems = refs[2 * count :]
    width = acc.shape[1]
    taps = weight.shape[0] // width
    half = (mine[0].shape[0] - hidden) // taps
    s, j = lax.axis_index("strand"), lax.axis_index("seq")
    copies = []
    for r, shard in enumerate(origins(block, s)):
        for q, (ref, part) in enumerate(((mine[r], s), (other[r], 1 - s))):
            start = pl.multiple_of((shard * 2 + part) * half, half)
            for tap in range(taps):
                copy = pltpu.make_async_copy(
                    ref.at[pl.ds(hidden + tap * half, half)],
                    weight.at[pl.ds(tap * width + start, half)],
                    sems.at[(r * 2 + q) * taps + tap],
                )
                copy.start()
                copies.append(copy)
    if parts > 1:
        size = states[0].shape[0]
        for k, state in enumerate(states):
            at = lax.rem(j + n - k, n)
            out[pl.ds(pl.multiple_of(at * size, size), size)] = state[...].astype(F32)
        state = out[...]
    else:
        state = states[0][...]
    normed = normalize(state, gain_ref[block : block + 1]).astype(BF16)
    shift = state.shape[0] // n * min(2**block, n // 2)
    for copy in copies:
        copy.wait()
    acc[...] = matmul_nt(normed, weight[width : 2 * width])
    acc[shift:] += matmul_nt(normed[:-shift], weight[:width])
    acc[:-shift] += matmul_nt(normed[shift:], weight[2 * width :])
    out[...] = state + acc[...].astype(BF16).astype(F32)


def conv(states, gain, mine, other, block, hidden, taps):
    width = gain.shape[1]
    rows = sum(v.shape[0] for v in states)
    arrays = len(mine) + len(other)
    return pl.pallas_call(
        functools.partial(conv_kernel, block, len(states), hidden),
        out_shape=jax.ShapeDtypeStruct((rows, width), F32),
        in_specs=[VMEM_SPEC] * (1 + len(states)) + [ANY_SPEC] * arrays,
        out_specs=VMEM_SPEC,
        scratch_shapes=[
            pltpu.VMEM((taps * width, width), BF16),
            pltpu.VMEM((rows, width), F32),
            pltpu.SemaphoreType.DMA((arrays * taps,)),
        ],
        compiler_params=PARAMS,
        name=f"conv{block}",
    )(gain, *states, *mine, *other)


def ff_kernel(block, first, ends, half, gain_ref, head_ref, state_ref, *refs):
    if not first:
        mixed_ref, refs = refs[0], refs[1:]
    outs = 1 if ends else 2
    count = (len(refs) - outs - 4) // 2
    mine, other = refs[:count], refs[count : 2 * count]
    out = refs[2 * count]
    up, down, hid, sems = refs[-4:]
    copies = []
    for r in range(count):
        for q, ref in enumerate((mine[r], other[r])):
            at = (2 * r + q) * half
            for w, to in enumerate((up, down)):
                copy = pltpu.make_async_copy(
                    ref.at[pl.ds(w * half, half)], to.at[pl.ds(at, half)], sems.at[(2 * r + q) * 2 + w]
                )
                copy.start()
                copies.append(copy)
    state = state_ref[...]
    if first:
        mixed = normalize(state, gain_ref[block : block + 1]).astype(BF16)
    else:
        mixed = mixed_ref[...]
    for r in range(count):
        for copy in copies[4 * r : 4 * r + 4]:
            copy.wait()
        part = slice(2 * r * half, 2 * (r + 1) * half)
        hid[:, part] = jax.nn.gelu(matmul_nt(mixed, up[part])).astype(BF16)
    state = state + matmul(hid[...], down[...])
    if ends == "head":
        state = normalize(state, head_ref[...]).astype(BF16)
    out[...] = state
    if not ends:
        refs[2 * count + 1][...] = mixed


def feed_forward(state, mixed, gain, head, mine, other, block, half, ends):
    rows, width = state.shape
    arrays = len(mine) + len(other)
    out = [jax.ShapeDtypeStruct((rows, width), BF16 if ends == "head" else F32)]
    if not ends:
        out.append(jax.ShapeDtypeStruct((rows, width), BF16))
    given = [state] if mixed is None else [state, mixed]
    return pl.pallas_call(
        functools.partial(ff_kernel, block, mixed is None, ends, half),
        out_shape=out,
        in_specs=[VMEM_SPEC] * (2 + len(given)) + [ANY_SPEC] * arrays,
        out_specs=[VMEM_SPEC] * len(out),
        scratch_shapes=[
            pltpu.VMEM((arrays * half, width), BF16),
            pltpu.VMEM((arrays * half, width), BF16),
            pltpu.VMEM((rows, arrays * half), BF16),
            pltpu.SemaphoreType.DMA((arrays * 2,)),
        ],
        compiler_params=PARAMS,
        name=f"ff{block}",
    )(gain, head, *given, *mine, *other)


def head_kernel(final_ref, opposite_ref, value_ref, gate_ref, out_ref, *refs):
    *outs, result = refs
    n = len(outs)
    size = outs[0].shape[0]
    j = lax.axis_index("seq")
    value = matmul(final_ref[...], value_ref[...])
    row = lax.broadcasted_iota(jnp.int32, (size, size), 0)
    col = lax.broadcasted_iota(jnp.int32, (size, size), 1)
    reverse = jnp.where(row + col == size - 1, 1.0, 0.0).astype(BF16)
    flipped = [
        matmul(reverse, opposite_ref[(n - 1 - i) * size : (n - i) * size]).astype(BF16) for i in range(n)
    ]
    mirrored = matmul(jnp.concatenate(flipped, 0), gate_ref[...]).astype(BF16)
    gated = (value * jax.nn.sigmoid(mirrored.astype(F32))).astype(BF16)
    result[...] = matmul(gated, out_ref[...]).astype(BF16)
    for k, out in enumerate(outs):
        at = lax.rem(j + k, n)
        out[...] = result[pl.ds(pl.multiple_of(at * size, size), size)]


def local_spread(
    seq_in, conv_norm, conv_weight, ff_norm, up_weight, down_weight,
    head_norm, value_weight, gate_weight, out_weight,
):
    n = lax.axis_size("seq")
    blocks, taps, width, _ = conv_weight.shape
    hidden = up_weight.shape[2]
    rows = seq_in.shape[1]
    part = jax.ShapeDtypeStruct((rows // n, width), BF16)
    halves = [pack(conv_weight, up_weight, down_weight, b) for b in range(blocks)]
    to = lambda k: (lambda g, i, s, c: (g, (i + k) % n, s, c if s == 0 else 1 - c))
    parts = pl.pallas_call(
        split_kernel, out_shape=[part] * n, in_specs=[VMEM_SPEC], out_specs=[VMEM_SPEC] * n,
        compiler_params=PARAMS, name="split",
    )(seq_in[0])
    states = [moved(p, to(k)) for k, p in enumerate(parts)]
    head = head_norm[None]
    for b, (mine, other) in enumerate(halves):
        a = gathered(mine, b)
        mine = [mine] + a
        other = [other] + [other_core(v) for v in a]
        state = conv(states, conv_norm, mine, other, b, hidden, taps)
        if b < blocks - 1:
            (state,) = feed_forward(state, None, ff_norm, head, mine, other, b, hidden // 2, "state")
        else:
            early = len(mine) // 2
            state, mixed = feed_forward(
                state, None, ff_norm, head, mine[:early], other[:early], b, hidden // 2, ""
            )
            (state,) = feed_forward(
                state, mixed, ff_norm, head, mine[early:], other[early:], b, hidden // 2, "head"
            )
        states = [state]
    opposite = other_core(state)
    results = pl.pallas_call(
        head_kernel, out_shape=[part] * n, in_specs=[VMEM_SPEC] * 5, out_specs=[VMEM_SPEC] * n,
        scratch_shapes=[pltpu.VMEM((rows, width), BF16)], compiler_params=PARAMS, name="head",
    )(state, opposite, value_weight, gate_weight, out_weight)
    home = [moved(r, to(k)) for k, r in enumerate(results)]
    joined = pl.pallas_call(
        join_kernel, out_shape=jax.ShapeDtypeStruct((rows, width), BF16), in_specs=[VMEM_SPEC] * n,
        out_specs=VMEM_SPEC, compiler_params=PARAMS, name="join",
    )(*home)
    return joined[None]


def solution(mesh):
    in_specs = (
        P("strand", ("groups", "seq", "chan"), None),
        P(),
        P(None, None, None, ("seq", "chan")),
        P(),
        P(None, None, ("seq", "chan")),
        P(None, ("seq", "chan"), None),
        P(),
        P(),
        P(),
        P(),
    )
    out_specs = P("strand", ("groups", "seq", "chan"), None)

    def step(seq_in, conv_norm, conv_weight, *rest):
        size = mesh.shape
        shards = size["seq"] * size["chan"]
        tiled = conv_weight.shape[3] % (32 * shards) == 0
        spread = tiled and (size["groups"], size["seq"], size["strand"], size["chan"]) == (2, 4, 2, 2)
        local = local_spread if spread else local_plain
        run = jax.shard_map(local, mesh=mesh, in_specs=in_specs, out_specs=out_specs, check_vma=False)
        return run(seq_in, conv_norm, conv_weight, *rest)

    return step
```

```python
import functools
import itertools

import jax
import jax.numpy as jnp
from jax import lax
from jax.experimental import pallas as pl
from jax.experimental.pallas import tpu as pltpu
from jax.sharding import PartitionSpec as P

AXES = ("groups", "seq", "strand", "chan")
BF16, F32 = jnp.bfloat16, jnp.float32
PARAMS = pltpu.CompilerParams(vmem_limit_bytes=40 * 2**20)
VMEM_SPEC = pl.BlockSpec(memory_space=pltpu.VMEM)


def normalize(values, gain):
    return values * lax.rsqrt(jnp.mean(values * values, axis=-1, keepdims=True) + 1e-06) * gain


def matmul(left, right):
    return jnp.dot(left, right, preferred_element_type=F32)


def matmul_nt(left, right):
    return lax.dot_general(left, right, (((1,), (1,)), ((), ())), preferred_element_type=F32)


def passed_along(value, axis, steps):
    count = lax.axis_size(axis)
    initial, last = (max(0, -steps), min(count, count - steps))
    return lax.ppermute(value, axis, [(source, source + steps) for source in range(initial, last)])


def swapped(x, axis, stride):
    return lax.ppermute(x, axis, [(i, i ^ 1 << stride) for i in range(lax.axis_size(axis))])


def local_plain(
    seq_in, conv_norm, conv_weight, ff_norm, up_weight, down_weight,
    head_norm, value_weight, gate_weight, out_weight,
):
    state = seq_in[0].astype(F32)
    seq_count = lax.axis_size("seq")
    for block in range(conv_weight.shape[0]):
        reach = min(2**block, seq_count // 2)
        normed = normalize(state, conv_norm[block]).astype(BF16)
        before = passed_along(normed, "seq", reach)
        after = passed_along(normed, "seq", -reach)
        piece = lax.all_gather(conv_weight[block], ("seq", "chan"), axis=2, tiled=True)
        total = matmul(before, piece[0]) + matmul(normed, piece[1]) + matmul(after, piece[2])
        state = state + total.astype(BF16).astype(F32)
        mixed = normalize(state, ff_norm[block]).astype(BF16)
        up = lax.all_gather(up_weight[block], ("seq", "chan"), axis=1, tiled=True)
        hidden = jax.nn.gelu(matmul(mixed, up)).astype(BF16)
        down = lax.all_gather(down_weight[block], ("seq", "chan"), axis=0, tiled=True)
        state = state + matmul(hidden, down)
    final = normalize(state, head_norm).astype(BF16)
    value = matmul(final, value_weight)
    bit_count = (seq_count * lax.axis_size("chan")).bit_length() - 1
    opposite = swapped(final, "strand", 0)
    for digit in range(bit_count):
        opposite = swapped(opposite, ("seq", "chan"), digit)
    opposite = jnp.flip(opposite, 0)
    mirrored = matmul(opposite, gate_weight).astype(BF16)
    gated = (value * jax.nn.sigmoid(mirrored.astype(F32))).astype(BF16)
    return matmul(gated, out_weight).astype(BF16)[None]


def moved(value, go):
    sizes = [lax.axis_size(a) for a in AXES]

    def flat(at):
        number = 0
        for n, k in zip(sizes, at):
            number = number * n + k
        return number

    pairs = [(flat(at), flat(go(*at))) for at in itertools.product(*map(range, sizes))]
    return lax.ppermute(value, AXES, pairs)


def across(value):
    return moved(value, lambda g, i, s, c: (g, i, s, 1 - c))


def planes(value):
    return moved(value, lambda g, i, s, c: (1 - g, i, s, c))


def other_core(value):
    return moved(value, lambda g, i, s, c: (g, i, 1 - s, c))


def along(value):
    n = lax.axis_size("seq")
    return moved(value, lambda g, i, s, c: (g, (i + 1 - 2 * g) % n, s, c))


def after(values, events):
    values, _ = lax.optimization_barrier((tuple(values), tuple(events)))
    return values


def origins():
    g, i, c = (lax.axis_index(a) for a in ("groups", "seq", "chan"))
    n, m = lax.axis_size("seq"), lax.axis_size("chan")
    a = lax.rem(i + n - 1 + 2 * g, n)
    b = lax.rem(i + 2, n)
    ya = lax.rem(i + n + 1 - 2 * g, n)
    x = 1 - c
    at = [(i, c), (a, c), (b, c), (i, x), (a, x), (b, x), (ya, c), (ya, x)]
    return [k * m + h for k, h in at]


def pack_kernel(plan, *refs):
    first = lax.axis_index("strand") == 0
    refs, mine_ref, other_ref = refs[:-2], refs[-2], refs[-1]
    at = 0
    for ref, block, turn in zip(refs, *plan):
        whole = ref[block].T if turn else ref[block]
        taps = whole[None] if whole.ndim == 2 else whole
        for tap in range(taps.shape[0]):
            half = taps.shape[1] // 2
            top, low = taps[tap, :half], taps[tap, half:]
            mine_ref[at : at + half] = jnp.where(first, top, low)
            other_ref[at : at + half] = jnp.where(first, low, top)
            at += half


def pack(arrays, blocks, turned, rows, name):
    shape = jax.ShapeDtypeStruct((rows, arrays[-1].shape[-1]), BF16)
    return pl.pallas_call(
        functools.partial(pack_kernel, (blocks, turned)),
        out_shape=[shape, shape],
        in_specs=[VMEM_SPEC] * len(arrays),
        out_specs=[VMEM_SPEC] * 2,
        compiler_params=PARAMS,
        name=name,
    )(*arrays)


def split_kernel(rows_ref, *out_refs):
    n = lax.axis_size("seq")
    i, s = lax.axis_index("seq"), lax.axis_index("strand")
    size = out_refs[0].shape[0]
    for k, out in enumerate(out_refs):
        j = lax.rem(i + k, n)
        sub = jnp.where(s == 0, j, n - 1 - j)
        out[...] = rows_ref[pl.ds(pl.multiple_of(sub * size, size), size)]


def join_kernel(*refs):
    *parts, out = refs
    n = lax.axis_size("seq")
    i, s = lax.axis_index("seq"), lax.axis_index("strand")
    size = parts[0].shape[0]
    for k, part in enumerate(parts):
        j = lax.rem(i + n - k, n)
        sub = jnp.where(s == 0, j, n - 1 - j)
        out[pl.ds(pl.multiple_of(sub * size, size), size)] = part[...]


def conv_kernel(block, parts, start, gain_ref, *refs):
    n = lax.axis_size("seq")
    states, refs = refs[:parts], refs[parts:]
    count = (len(refs) - 3) // 2
    mine, other = refs[:count], refs[count : 2 * count]
    out, weight, acc = refs[2 * count :]
    width = acc.shape[1]
    taps = weight.shape[0] // width
    half = width // count // 2
    s, j = lax.axis_index("strand"), lax.axis_index("seq")
    for r, shard in enumerate(origins()):
        for ref, part in ((mine[r], s), (other[r], 1 - s)):
            at = pl.multiple_of((shard * 2 + part) * half, half)
            for tap in range(taps):
                weight[pl.ds(tap * width + at, half)] = ref[start + tap * half : start + (tap + 1) * half]
    if parts > 1:
        size = states[0].shape[0]
        for k, state in enumerate(states):
            at = lax.rem(j + n - k, n)
            out[pl.ds(pl.multiple_of(at * size, size), size)] = state[...].astype(F32)
        state = out[...]
    else:
        state = states[0][...]
    normed = normalize(state, gain_ref[block : block + 1]).astype(BF16)
    shift = state.shape[0] // n * min(2**block, n // 2)
    acc[...] = matmul_nt(normed, weight[width : 2 * width])
    acc[shift:] += matmul_nt(normed[:-shift], weight[:width])
    acc[:-shift] += matmul_nt(normed[shift:], weight[2 * width :])
    out[...] = state + acc[...].astype(BF16).astype(F32)


def conv(states, gain, mine, other, block, start, taps):
    width = gain.shape[1]
    rows = sum(v.shape[0] for v in states)
    arrays = len(mine) + len(other)
    return pl.pallas_call(
        functools.partial(conv_kernel, block, len(states), start),
        out_shape=jax.ShapeDtypeStruct((rows, width), F32),
        in_specs=[VMEM_SPEC] * (1 + len(states) + arrays),
        out_specs=VMEM_SPEC,
        scratch_shapes=[pltpu.VMEM((taps * width, width), BF16), pltpu.VMEM((rows, width), F32)],
        compiler_params=PARAMS,
        name=f"conv{block}",
    )(gain, *states, *mine, *other)


def ff_kernel(block, first, ends, half, gain_ref, head_ref, state_ref, *refs):
    if not first:
        mixed_ref, refs = refs[0], refs[1:]
    outs = 1 if ends else 2
    count = (len(refs) - outs - 1) // 2
    mine, other = refs[:count], refs[count : 2 * count]
    out, hid = refs[2 * count], refs[-1]
    state = state_ref[...]
    if first:
        mixed = normalize(state, gain_ref[block : block + 1]).astype(BF16)
    else:
        mixed = mixed_ref[...]
    down = []
    for r in range(count):
        up = jnp.concatenate([mine[r][:half], other[r][:half]], 0)
        hid[:, 2 * r * half : 2 * (r + 1) * half] = jax.nn.gelu(matmul_nt(mixed, up)).astype(BF16)
        down += [mine[r][half : 2 * half], other[r][half : 2 * half]]
    state = state + matmul(hid[...], jnp.concatenate(down, 0))
    if ends == "head":
        state = normalize(state, head_ref[...]).astype(BF16)
    out[...] = state
    if not ends:
        refs[2 * count + 1][...] = mixed


def feed_forward(state, mixed, gain, head, mine, other, block, half, ends):
    rows, width = state.shape
    arrays = len(mine) + len(other)
    out = [jax.ShapeDtypeStruct((rows, width), BF16 if ends == "head" else F32)]
    if not ends:
        out.append(jax.ShapeDtypeStruct((rows, width), BF16))
    given = [state] if mixed is None else [state, mixed]
    return pl.pallas_call(
        functools.partial(ff_kernel, block, mixed is None, ends, half),
        out_shape=out,
        in_specs=[VMEM_SPEC] * (2 + len(given) + arrays),
        out_specs=[VMEM_SPEC] * len(out),
        scratch_shapes=[pltpu.VMEM((rows, arrays * half), BF16)],
        compiler_params=PARAMS,
        name=f"ff{block}",
    )(gain, head, *given, *mine, *other)


def head_kernel(final_ref, opposite_ref, value_ref, gate_ref, out_ref, *refs):
    *outs, result = refs
    n = len(outs)
    size = outs[0].shape[0]
    j = lax.axis_index("seq")
    value = matmul(final_ref[...], value_ref[...])
    row = lax.broadcasted_iota(jnp.int32, (size, size), 0)
    col = lax.broadcasted_iota(jnp.int32, (size, size), 1)
    reverse = jnp.where(row + col == size - 1, 1.0, 0.0).astype(BF16)
    flipped = [
        matmul(reverse, opposite_ref[(n - 1 - i) * size : (n - i) * size]).astype(BF16) for i in range(n)
    ]
    mirrored = matmul(jnp.concatenate(flipped, 0), gate_ref[...]).astype(BF16)
    gated = (value * jax.nn.sigmoid(mirrored.astype(F32))).astype(BF16)
    result[...] = matmul(gated, out_ref[...]).astype(BF16)
    for k, out in enumerate(outs):
        at = lax.rem(j + k, n)
        out[...] = result[pl.ds(pl.multiple_of(at * size, size), size)]


def local_spread(
    seq_in, conv_norm, conv_weight, ff_norm, up_weight, down_weight,
    head_norm, value_weight, gate_weight, out_weight,
):
    n = lax.axis_size("seq")
    blocks, taps, width, chans = conv_weight.shape
    hidden = up_weight.shape[2]
    half = hidden // 2
    rows = seq_in.shape[1]
    part = jax.ShapeDtypeStruct((rows // n, width), BF16)
    turned = jnp.swapaxes(conv_weight, 2, 3)
    mine0, other0 = pack(
        (up_weight, down_weight, turned, turned), (0, 0, 0, 1), (True, False, False, False),
        hidden + taps * chans, "pack0",
    )
    mine1, other1 = pack((up_weight, down_weight), (1, 1), (True, False), hidden, "pack1")
    to = lambda k: (lambda g, i, s, c: (g, (i + k) % n, s, c if s == 0 else 1 - c))
    parts = pl.pallas_call(
        split_kernel, out_shape=[part] * n, in_specs=[VMEM_SPEC], out_specs=[VMEM_SPEC] * n,
        compiler_params=PARAMS, name="split",
    )(seq_in[0])

    a0 = along(mine0)
    x0 = across(mine0)
    b0 = along(a0)
    xa0 = across(a0)
    ya0 = planes(a0)
    parts = after(parts, [b0])
    states = [moved(p, to(k)) for k, p in enumerate(parts)]
    xb0 = across(b0)
    yxa0 = planes(xa0)
    (own1,) = after([mine1], [b0])
    a1 = along(own1)
    (own1x,) = after([mine1], [xb0])
    x1 = across(own1x)
    b1 = along(a1)
    xa1 = across(a1)
    ya1 = planes(a1)
    xb1 = across(b1)
    yxa1 = planes(xa1)

    got0 = [a0, b0, x0, xa0, xb0, ya0, yxa0]
    got1 = [a1, b1, x1, xa1, xb1, ya1, yxa1]
    mine_0, other_0 = [mine0] + got0, [other0] + [other_core(v) for v in got0]
    mine_1, other_1 = [mine1] + got1, [other1] + [other_core(v) for v in got1]
    head = head_norm[None]
    state = conv(states, conv_norm, mine_0, other_0, 0, hidden, taps)
    (state,) = feed_forward(state, None, ff_norm, head, mine_0, other_0, 0, half, "state")
    state = conv([state], conv_norm, mine_0, other_0, 1, hidden + taps * chans // 2, taps)
    early, late = (0, 1, 2, 3, 6), (4, 5, 7)
    pick = lambda values, which: [values[k] for k in which]
    state, mixed = feed_forward(
        state, None, ff_norm, head, pick(mine_1, early), pick(other_1, early), 1, half, ""
    )
    (final,) = feed_forward(
        state, mixed, ff_norm, head, pick(mine_1, late), pick(other_1, late), 1, half, "head"
    )
    opposite = other_core(final)
    results = pl.pallas_call(
        head_kernel, out_shape=[part] * n, in_specs=[VMEM_SPEC] * 5, out_specs=[VMEM_SPEC] * n,
        scratch_shapes=[pltpu.VMEM((rows, width), BF16)], compiler_params=PARAMS, name="head",
    )(final, opposite, value_weight, gate_weight, out_weight)
    home = [moved(r, to(k)) for k, r in enumerate(results)]
    joined = pl.pallas_call(
        join_kernel, out_shape=jax.ShapeDtypeStruct((rows, width), BF16), in_specs=[VMEM_SPEC] * n,
        out_specs=VMEM_SPEC, compiler_params=PARAMS, name="join",
    )(*home)
    return joined[None]


def solution(mesh):
    in_specs = (
        P("strand", ("groups", "seq", "chan"), None),
        P(),
        P(None, None, None, ("seq", "chan")),
        P(),
        P(None, None, ("seq", "chan")),
        P(None, ("seq", "chan"), None),
        P(),
        P(),
        P(),
        P(),
    )
    out_specs = P("strand", ("groups", "seq", "chan"), None)

    def step(seq_in, conv_norm, conv_weight, *rest):
        size = mesh.shape
        shards = size["seq"] * size["chan"]
        tiled = conv_weight.shape[3] % (32 * shards) == 0
        blocks = conv_weight.shape[0]
        spread = tiled and blocks == 2 and [size[a] for a in AXES] == [2, 4, 2, 2]
        local = local_spread if spread else local_plain
        run = jax.shard_map(local, mesh=mesh, in_specs=in_specs, out_specs=out_specs, check_vma=False)
        return run(seq_in, conv_norm, conv_weight, *rest)

    return step
```

```python
import functools
import itertools

import jax
import jax.numpy as jnp
from jax import lax
from jax.experimental import pallas as pl
from jax.experimental.pallas import tpu as pltpu
from jax.sharding import PartitionSpec as P

AXES = ("groups", "seq", "strand", "chan")
BF16, F32 = jnp.bfloat16, jnp.float32
PARAMS = pltpu.CompilerParams(vmem_limit_bytes=40 * 2**20)
VMEM_SPEC = pl.BlockSpec(memory_space=pltpu.VMEM)


def normalize(values, gain):
    return values * lax.rsqrt(jnp.mean(values * values, axis=-1, keepdims=True) + 1e-06) * gain


def matmul(left, right):
    return jnp.dot(left, right, preferred_element_type=F32)


def matmul_nt(left, right):
    return lax.dot_general(left, right, (((1,), (1,)), ((), ())), preferred_element_type=F32)


def passed_along(value, axis, steps):
    count = lax.axis_size(axis)
    initial, last = (max(0, -steps), min(count, count - steps))
    return lax.ppermute(value, axis, [(source, source + steps) for source in range(initial, last)])


def swapped(x, axis, stride):
    return lax.ppermute(x, axis, [(i, i ^ 1 << stride) for i in range(lax.axis_size(axis))])


def local_plain(
    seq_in, conv_norm, conv_weight, ff_norm, up_weight, down_weight,
    head_norm, value_weight, gate_weight, out_weight,
):
    state = seq_in[0].astype(F32)
    seq_count = lax.axis_size("seq")
    for block in range(conv_weight.shape[0]):
        reach = min(2**block, seq_count // 2)
        normed = normalize(state, conv_norm[block]).astype(BF16)
        before = passed_along(normed, "seq", reach)
        after = passed_along(normed, "seq", -reach)
        piece = lax.all_gather(conv_weight[block], ("seq", "chan"), axis=2, tiled=True)
        total = matmul(before, piece[0]) + matmul(normed, piece[1]) + matmul(after, piece[2])
        state = state + total.astype(BF16).astype(F32)
        mixed = normalize(state, ff_norm[block]).astype(BF16)
        up = lax.all_gather(up_weight[block], ("seq", "chan"), axis=1, tiled=True)
        hidden = jax.nn.gelu(matmul(mixed, up)).astype(BF16)
        down = lax.all_gather(down_weight[block], ("seq", "chan"), axis=0, tiled=True)
        state = state + matmul(hidden, down)
    final = normalize(state, head_norm).astype(BF16)
    value = matmul(final, value_weight)
    bit_count = (seq_count * lax.axis_size("chan")).bit_length() - 1
    opposite = swapped(final, "strand", 0)
    for digit in range(bit_count):
        opposite = swapped(opposite, ("seq", "chan"), digit)
    opposite = jnp.flip(opposite, 0)
    mirrored = matmul(opposite, gate_weight).astype(BF16)
    gated = (value * jax.nn.sigmoid(mirrored.astype(F32))).astype(BF16)
    return matmul(gated, out_weight).astype(BF16)[None]


def moved(value, go):
    sizes = [lax.axis_size(a) for a in AXES]

    def flat(at):
        number = 0
        for n, k in zip(sizes, at):
            number = number * n + k
        return number

    pairs = [(flat(at), flat(go(*at))) for at in itertools.product(*map(range, sizes))]
    return lax.ppermute(value, AXES, pairs)


def across(value):
    return moved(value, lambda g, i, s, c: (g, i, s, 1 - c))


def planes(value):
    return moved(value, lambda g, i, s, c: (1 - g, i, s, c))


def other_core(value):
    return moved(value, lambda g, i, s, c: (g, i, 1 - s, c))


def along(value):
    n = lax.axis_size("seq")
    return moved(value, lambda g, i, s, c: (g, (i + 1 - 2 * g) % n, s, c))


def after(values, events):
    values, _ = lax.optimization_barrier((tuple(values), tuple(events)))
    return values


def origins():
    g, i, c = (lax.axis_index(a) for a in ("groups", "seq", "chan"))
    n, m = lax.axis_size("seq"), lax.axis_size("chan")
    a = lax.rem(i + n - 1 + 2 * g, n)
    b = lax.rem(i + 2, n)
    ya = lax.rem(i + n + 1 - 2 * g, n)
    x = 1 - c
    at = [(i, c), (a, c), (b, c), (i, x), (a, x), (b, x), (ya, c), (ya, x)]
    return [k * m + h for k, h in at]


def pack_kernel(plan, *refs):
    first = lax.axis_index("strand") == 0
    refs, mine_ref, other_ref = refs[:-2], refs[-2], refs[-1]
    at = 0
    for ref, block, turn in zip(refs, *plan):
        whole = ref[block].T if turn else ref[block]
        taps = whole[None] if whole.ndim == 2 else whole
        for tap in range(taps.shape[0]):
            half = taps.shape[1] // 2
            top, low = taps[tap, :half], taps[tap, half:]
            mine_ref[at : at + half] = jnp.where(first, top, low)
            other_ref[at : at + half] = jnp.where(first, low, top)
            at += half


def pack(arrays, blocks, turned, rows, name):
    shape = jax.ShapeDtypeStruct((rows, arrays[-1].shape[-1]), BF16)
    return pl.pallas_call(
        functools.partial(pack_kernel, (blocks, turned)),
        out_shape=[shape, shape],
        in_specs=[VMEM_SPEC] * len(arrays),
        out_specs=[VMEM_SPEC] * 2,
        compiler_params=PARAMS,
        name=name,
    )(*arrays)


def split_kernel(rows_ref, *out_refs):
    n = lax.axis_size("seq")
    i, s = lax.axis_index("seq"), lax.axis_index("strand")
    size = out_refs[0].shape[0]
    for k, out in enumerate(out_refs):
        j = lax.rem(i + k, n)
        sub = jnp.where(s == 0, j, n - 1 - j)
        out[...] = rows_ref[pl.ds(pl.multiple_of(sub * size, size), size)]


def join_kernel(*refs):
    *parts, out = refs
    n = lax.axis_size("seq")
    i, s = lax.axis_index("seq"), lax.axis_index("strand")
    size = parts[0].shape[0]
    for k, part in enumerate(parts):
        j = lax.rem(i + n - k, n)
        sub = jnp.where(s == 0, j, n - 1 - j)
        out[pl.ds(pl.multiple_of(sub * size, size), size)] = part[...]


def conv_kernel(block, parts, start, gain_ref, *refs):
    n = lax.axis_size("seq")
    states, refs = refs[:parts], refs[parts:]
    count = (len(refs) - 3) // 2
    mine, other = refs[:count], refs[count : 2 * count]
    out, weight, acc = refs[2 * count :]
    width = acc.shape[1]
    taps = weight.shape[0] // width
    half = width // count // 2
    s, j = lax.axis_index("strand"), lax.axis_index("seq")
    for r, shard in enumerate(origins()):
        for ref, part in ((mine[r], s), (other[r], 1 - s)):
            at = pl.multiple_of((shard * 2 + part) * half, half)
            for tap in range(taps):
                weight[pl.ds(tap * width + at, half)] = ref[start + tap * half : start + (tap + 1) * half]
    if parts > 1:
        size = states[0].shape[0]
        for k, state in enumerate(states):
            at = lax.rem(j + n - k, n)
            out[pl.ds(pl.multiple_of(at * size, size), size)] = state[...].astype(F32)
        state = out[...]
    else:
        state = states[0][...]
    normed = normalize(state, gain_ref[block : block + 1]).astype(BF16)
    shift = state.shape[0] // n * min(2**block, n // 2)
    acc[...] = matmul_nt(normed, weight[width : 2 * width])
    acc[shift:] += matmul_nt(normed[:-shift], weight[:width])
    acc[:-shift] += matmul_nt(normed[shift:], weight[2 * width :])
    out[...] = state + acc[...].astype(BF16).astype(F32)


def conv(states, gain, mine, other, block, start, taps):
    width = gain.shape[1]
    rows = sum(v.shape[0] for v in states)
    arrays = len(mine) + len(other)
    return pl.pallas_call(
        functools.partial(conv_kernel, block, len(states), start),
        out_shape=jax.ShapeDtypeStruct((rows, width), F32),
        in_specs=[VMEM_SPEC] * (1 + len(states) + arrays),
        out_specs=VMEM_SPEC,
        scratch_shapes=[pltpu.VMEM((taps * width, width), BF16), pltpu.VMEM((rows, width), F32)],
        compiler_params=PARAMS,
        name=f"conv{block}",
    )(gain, *states, *mine, *other)


def ff_kernel(block, first, ends, start, half, gain_ref, head_ref, state_ref, *refs):
    if not first:
        mixed_ref, refs = refs[0], refs[1:]
    outs = 1 if ends else 2
    count = (len(refs) - outs - 1) // 2
    mine, other = refs[:count], refs[count : 2 * count]
    out, hid = refs[2 * count], refs[-1]
    state = state_ref[...]
    if first:
        mixed = normalize(state, gain_ref[block : block + 1]).astype(BF16)
    else:
        mixed = mixed_ref[...]
    down = []
    for r in range(count):
        up = jnp.concatenate([v[r][start : start + half] for v in (mine, other)], 0)
        hid[:, 2 * r * half : 2 * (r + 1) * half] = jax.nn.gelu(matmul_nt(mixed, up)).astype(BF16)
        down += [v[r][start + half : start + 2 * half] for v in (mine, other)]
    state = state + matmul(hid[...], jnp.concatenate(down, 0))
    if ends == "head":
        state = normalize(state, head_ref[...]).astype(BF16)
    out[...] = state
    if not ends:
        refs[2 * count + 1][...] = mixed


def feed_forward(state, mixed, gain, head, mine, other, block, start, half, ends):
    rows, width = state.shape
    arrays = len(mine) + len(other)
    out = [jax.ShapeDtypeStruct((rows, width), BF16 if ends == "head" else F32)]
    if not ends:
        out.append(jax.ShapeDtypeStruct((rows, width), BF16))
    given = [state] if mixed is None else [state, mixed]
    return pl.pallas_call(
        functools.partial(ff_kernel, block, mixed is None, ends, start, half),
        out_shape=out,
        in_specs=[VMEM_SPEC] * (2 + len(given) + arrays),
        out_specs=[VMEM_SPEC] * len(out),
        scratch_shapes=[pltpu.VMEM((rows, arrays * half), BF16)],
        compiler_params=PARAMS,
        name=f"ff{block}",
    )(gain, head, *given, *mine, *other)


def head_kernel(final_ref, opposite_ref, value_ref, gate_ref, out_ref, *refs):
    *outs, result = refs
    n = len(outs)
    size = outs[0].shape[0]
    j = lax.axis_index("seq")
    value = matmul(final_ref[...], value_ref[...])
    row = lax.broadcasted_iota(jnp.int32, (size, size), 0)
    col = lax.broadcasted_iota(jnp.int32, (size, size), 1)
    reverse = jnp.where(row + col == size - 1, 1.0, 0.0).astype(BF16)
    flipped = [
        matmul(reverse, opposite_ref[(n - 1 - i) * size : (n - i) * size]).astype(BF16) for i in range(n)
    ]
    mirrored = matmul(jnp.concatenate(flipped, 0), gate_ref[...]).astype(BF16)
    gated = (value * jax.nn.sigmoid(mirrored.astype(F32))).astype(BF16)
    result[...] = matmul(gated, out_ref[...]).astype(BF16)
    for k, out in enumerate(outs):
        at = lax.rem(j + k, n)
        out[...] = result[pl.ds(pl.multiple_of(at * size, size), size)]


def local_spread(
    seq_in, conv_norm, conv_weight, ff_norm, up_weight, down_weight,
    head_norm, value_weight, gate_weight, out_weight,
):
    n = lax.axis_size("seq")
    blocks, taps, width, chans = conv_weight.shape
    hidden = up_weight.shape[2]
    half = hidden // 2
    rows = seq_in.shape[1]
    part = jax.ShapeDtypeStruct((rows // n, width), BF16)
    turned = jnp.swapaxes(conv_weight, 2, 3)
    cut = hidden + taps * chans
    own, own_other = pack(
        (up_weight, down_weight, turned, turned, up_weight, down_weight),
        (0, 0, 0, 1, 1, 1), (True, False, False, False, True, False), cut + hidden, "pack",
    )
    to = lambda k: (lambda g, i, s, c: (g, (i + k) % n, s, c if s == 0 else 1 - c))
    parts = pl.pallas_call(
        split_kernel, out_shape=[part] * n, in_specs=[VMEM_SPEC], out_specs=[VMEM_SPEC] * n,
        compiler_params=PARAMS, name="split",
    )(seq_in[0])

    a = along(own)
    x = across(own)
    b = along(a)
    xa = across(a)
    ya = planes(a)
    xb = across(b)
    yxa = planes(xa)
    parts = after(parts, [b])
    states = [moved(p, to(k)) for k, p in enumerate(parts)]
    mine = [own, a, b, x, xa, xb, ya, yxa]
    other = [own_other] + [other_core(v) for v in mine[1:]]
    head = head_norm[None]
    state = conv(states, conv_norm, mine, other, 0, hidden, taps)
    (state,) = feed_forward(state, None, ff_norm, head, mine, other, 0, 0, half, "state")
    state = conv([state], conv_norm, mine, other, 1, hidden + taps * chans // 2, taps)
    (final,) = feed_forward(state, None, ff_norm, head, mine, other, 1, cut, half, "head")
    opposite = other_core(final)
    results = pl.pallas_call(
        head_kernel, out_shape=[part] * n, in_specs=[VMEM_SPEC] * 5, out_specs=[VMEM_SPEC] * n,
        scratch_shapes=[pltpu.VMEM((rows, width), BF16)], compiler_params=PARAMS, name="head",
    )(final, opposite, value_weight, gate_weight, out_weight)
    home = [moved(r, to(k)) for k, r in enumerate(results)]
    joined = pl.pallas_call(
        join_kernel, out_shape=jax.ShapeDtypeStruct((rows, width), BF16), in_specs=[VMEM_SPEC] * n,
        out_specs=VMEM_SPEC, compiler_params=PARAMS, name="join",
    )(*home)
    return joined[None]


def solution(mesh):
    in_specs = (
        P("strand", ("groups", "seq", "chan"), None),
        P(),
        P(None, None, None, ("seq", "chan")),
        P(),
        P(None, None, ("seq", "chan")),
        P(None, ("seq", "chan"), None),
        P(),
        P(),
        P(),
        P(),
    )
    out_specs = P("strand", ("groups", "seq", "chan"), None)

    def step(seq_in, conv_norm, conv_weight, *rest):
        size = mesh.shape
        shards = size["seq"] * size["chan"]
        tiled = conv_weight.shape[3] % (32 * shards) == 0
        blocks = conv_weight.shape[0]
        spread = tiled and blocks == 2 and [size[a] for a in AXES] == [2, 4, 2, 2]
        local = local_spread if spread else local_plain
        run = jax.shard_map(local, mesh=mesh, in_specs=in_specs, out_specs=out_specs, check_vma=False)
        return run(seq_in, conv_norm, conv_weight, *rest)

    return step
```

```python
import functools
import itertools

import jax
import jax.numpy as jnp
from jax import lax
from jax.experimental import pallas as pl
from jax.experimental.pallas import tpu as pltpu
from jax.sharding import PartitionSpec as P

AXES = ("groups", "seq", "strand", "chan")
BF16, F32 = jnp.bfloat16, jnp.float32
PARAMS = pltpu.CompilerParams(vmem_limit_bytes=40 * 2**20)
VMEM_SPEC = pl.BlockSpec(memory_space=pltpu.VMEM)


def normalize(values, gain):
    return values * lax.rsqrt(jnp.mean(values * values, axis=-1, keepdims=True) + 1e-06) * gain


def matmul(left, right):
    return jnp.dot(left, right, preferred_element_type=F32)


def matmul_nt(left, right):
    return lax.dot_general(left, right, (((1,), (1,)), ((), ())), preferred_element_type=F32)


def passed_along(value, axis, steps):
    count = lax.axis_size(axis)
    initial, last = (max(0, -steps), min(count, count - steps))
    return lax.ppermute(value, axis, [(source, source + steps) for source in range(initial, last)])


def swapped(x, axis, stride):
    return lax.ppermute(x, axis, [(i, i ^ 1 << stride) for i in range(lax.axis_size(axis))])


def local_plain(
    seq_in, conv_norm, conv_weight, ff_norm, up_weight, down_weight,
    head_norm, value_weight, gate_weight, out_weight,
):
    state = seq_in[0].astype(F32)
    seq_count = lax.axis_size("seq")
    for block in range(conv_weight.shape[0]):
        reach = min(2**block, seq_count // 2)
        normed = normalize(state, conv_norm[block]).astype(BF16)
        before = passed_along(normed, "seq", reach)
        after = passed_along(normed, "seq", -reach)
        piece = lax.all_gather(conv_weight[block], ("seq", "chan"), axis=2, tiled=True)
        total = matmul(before, piece[0]) + matmul(normed, piece[1]) + matmul(after, piece[2])
        state = state + total.astype(BF16).astype(F32)
        mixed = normalize(state, ff_norm[block]).astype(BF16)
        up = lax.all_gather(up_weight[block], ("seq", "chan"), axis=1, tiled=True)
        hidden = jax.nn.gelu(matmul(mixed, up)).astype(BF16)
        down = lax.all_gather(down_weight[block], ("seq", "chan"), axis=0, tiled=True)
        state = state + matmul(hidden, down)
    final = normalize(state, head_norm).astype(BF16)
    value = matmul(final, value_weight)
    bit_count = (seq_count * lax.axis_size("chan")).bit_length() - 1
    opposite = swapped(final, "strand", 0)
    for digit in range(bit_count):
        opposite = swapped(opposite, ("seq", "chan"), digit)
    opposite = jnp.flip(opposite, 0)
    mirrored = matmul(opposite, gate_weight).astype(BF16)
    gated = (value * jax.nn.sigmoid(mirrored.astype(F32))).astype(BF16)
    return matmul(gated, out_weight).astype(BF16)[None]


def moved(value, go):
    sizes = [lax.axis_size(a) for a in AXES]

    def flat(at):
        number = 0
        for n, k in zip(sizes, at):
            number = number * n + k
        return number

    pairs = [(flat(at), flat(go(*at))) for at in itertools.product(*map(range, sizes))]
    return lax.ppermute(value, AXES, pairs)


def across(value):
    return moved(value, lambda g, i, s, c: (g, i, s, 1 - c))


def planes(value):
    return moved(value, lambda g, i, s, c: (1 - g, i, s, c))


def other_core(value):
    return moved(value, lambda g, i, s, c: (g, i, 1 - s, c))


def along(value):
    n = lax.axis_size("seq")
    return moved(value, lambda g, i, s, c: (g, (i + 1 - 2 * g) % n, s, c))


def after(values, events):
    values, _ = lax.optimization_barrier((tuple(values), tuple(events)))
    return values


def origins():
    g, i, c = (lax.axis_index(a) for a in ("groups", "seq", "chan"))
    n, m = lax.axis_size("seq"), lax.axis_size("chan")
    a = lax.rem(i + n - 1 + 2 * g, n)
    b = lax.rem(i + 2, n)
    ya = lax.rem(i + n + 1 - 2 * g, n)
    x = 1 - c
    at = [(i, c), (a, c), (b, c), (i, x), (a, x), (b, x), (ya, c), (ya, x)]
    return [k * m + h for k, h in at]


def pack_kernel(plan, mine, *refs):
    blocks, turned = plan
    refs, (out, wide, sems) = refs[:-3], refs[-3:]
    s = lax.axis_index("strand")
    part = s if mine else 1 - s
    at, turns, copies = 0, [], []

    def copy(source, target):
        copies.append(pltpu.make_async_copy(source, target, sems.at[len(copies)]))
        copies[-1].start()

    for ref, block, turn in zip(refs, blocks, turned):
        if turn:
            half = ref.shape[2] // 2
            columns = pl.ds(pl.multiple_of(part * half, half), half)
            copy(ref.at[block, :, columns], wide.at[len(turns)])
            turns.append((at, half, copies[-1]))
            at += half
        else:
            half = ref.shape[-2] // 2
            rows = pl.ds(pl.multiple_of(part * half, half), half)
            for tap in range(ref.shape[1]) if len(ref.shape) == 4 else (None,):
                source = ref.at[block, rows] if tap is None else ref.at[block, tap, rows]
                copy(source, out.at[at : at + half])
                at += half
    for k, (at, half, done) in enumerate(turns):
        done.wait()
        out[at : at + half] = wide[k].T
    for done in copies:
        if all(done is not turn[2] for turn in turns):
            done.wait()


def pack(arrays, blocks, turned, rows, mine):
    width = arrays[0].shape[1]
    half = arrays[0].shape[2] // 2
    return pl.pallas_call(
        functools.partial(pack_kernel, (blocks, turned), mine),
        out_shape=jax.ShapeDtypeStruct((rows, width), BF16),
        in_specs=[pl.BlockSpec(memory_space=pltpu.HBM)] * len(arrays),
        out_specs=VMEM_SPEC,
        scratch_shapes=[
            pltpu.VMEM((sum(turned), width, half), BF16),
            pltpu.SemaphoreType.DMA((2 * rows // 32,)),
        ],
        compiler_params=PARAMS,
        name="pack_own" if mine else "pack_rest",
    )(*[pltpu.with_memory_space_constraint(v, pltpu.HBM) for v in arrays])


def split_kernel(rows_ref, *out_refs):
    n = lax.axis_size("seq")
    i, s = lax.axis_index("seq"), lax.axis_index("strand")
    size = out_refs[0].shape[0]
    for k, out in enumerate(out_refs):
        j = lax.rem(i + k, n)
        sub = jnp.where(s == 0, j, n - 1 - j)
        out[...] = rows_ref[pl.ds(pl.multiple_of(sub * size, size), size)]


def join_kernel(*refs):
    *parts, out = refs
    n = lax.axis_size("seq")
    i, s = lax.axis_index("seq"), lax.axis_index("strand")
    size = parts[0].shape[0]
    for k, part in enumerate(parts):
        j = lax.rem(i + n - k, n)
        sub = jnp.where(s == 0, j, n - 1 - j)
        out[pl.ds(pl.multiple_of(sub * size, size), size)] = part[...]


def conv_kernel(block, parts, places, start, gain_ref, *refs):
    n = lax.axis_size("seq")
    states, arrays = refs[:parts], refs[parts:-3]
    out, weight, acc = refs[-3:]
    width = acc.shape[1]
    taps = weight.shape[0] // width
    half = width // len(places[0]) // 2
    s, j = lax.axis_index("strand"), lax.axis_index("seq")
    for side, part in zip(places, (s, 1 - s)):
        for (k, row), shard in zip(side, origins()):
            at = pl.multiple_of((shard * 2 + part) * half, half)
            for tap in range(taps):
                first = row + start + tap * half
                weight[pl.ds(tap * width + at, half)] = arrays[k][first : first + half]
    if parts > 1:
        size = states[0].shape[0]
        for k, state in enumerate(states):
            at = lax.rem(j + n - k, n)
            out[pl.ds(pl.multiple_of(at * size, size), size)] = state[...].astype(F32)
        state = out[...]
    else:
        state = states[0][...]
    normed = normalize(state, gain_ref[block : block + 1]).astype(BF16)
    shift = state.shape[0] // n * min(2**block, n // 2)
    acc[...] = matmul_nt(normed, weight[width : 2 * width])
    acc[shift:] += matmul_nt(normed[:-shift], weight[:width])
    acc[:-shift] += matmul_nt(normed[shift:], weight[2 * width :])
    out[...] = state + acc[...].astype(BF16).astype(F32)


def conv(states, gain, arrays, places, block, start, taps):
    width = gain.shape[1]
    rows = sum(v.shape[0] for v in states)
    return pl.pallas_call(
        functools.partial(conv_kernel, block, len(states), places, start),
        out_shape=jax.ShapeDtypeStruct((rows, width), F32),
        in_specs=[VMEM_SPEC] * (1 + len(states) + len(arrays)),
        out_specs=VMEM_SPEC,
        scratch_shapes=[pltpu.VMEM((taps * width, width), BF16), pltpu.VMEM((rows, width), F32)],
        compiler_params=PARAMS,
        name=f"conv{block}",
    )(gain, *states, *arrays)


def ff_kernel(block, first, ends, places, start, half, gain_ref, head_ref, state_ref, *refs):
    if not first:
        mixed_ref, refs = refs[0], refs[1:]
    arrays, out, hid = refs, refs[-2 if ends else -3], refs[-1]
    state = state_ref[...]
    if first:
        mixed = normalize(state, gain_ref[block : block + 1]).astype(BF16)
    else:
        mixed = mixed_ref[...]
    down = []
    for r, pair in enumerate(zip(*places)):
        up = jnp.concatenate([arrays[k][row + start : row + start + half] for k, row in pair], 0)
        hid[:, 2 * r * half : 2 * (r + 1) * half] = jax.nn.gelu(matmul_nt(mixed, up)).astype(BF16)
        down += [arrays[k][row + start + half : row + start + 2 * half] for k, row in pair]
    state = state + matmul(hid[...], jnp.concatenate(down, 0))
    if ends == "head":
        state = normalize(state, head_ref[...]).astype(BF16)
    out[...] = state
    if not ends:
        refs[-2][...] = mixed


def feed_forward(state, mixed, gain, head, arrays, places, block, start, half, ends):
    rows, width = state.shape
    out = [jax.ShapeDtypeStruct((rows, width), BF16 if ends == "head" else F32)]
    if not ends:
        out.append(jax.ShapeDtypeStruct((rows, width), BF16))
    given = [state] if mixed is None else [state, mixed]
    return pl.pallas_call(
        functools.partial(ff_kernel, block, mixed is None, ends, places, start, half),
        out_shape=out,
        in_specs=[VMEM_SPEC] * (2 + len(given) + len(arrays)),
        out_specs=[VMEM_SPEC] * len(out),
        scratch_shapes=[pltpu.VMEM((rows, 2 * len(places[0]) * half), BF16)],
        compiler_params=PARAMS,
        name=f"ff{block}",
    )(gain, head, *given, *arrays)


def head_kernel(final_ref, opposite_ref, value_ref, gate_ref, out_ref, *refs):
    *outs, result = refs
    n = len(outs)
    size = outs[0].shape[0]
    j = lax.axis_index("seq")
    value = matmul(final_ref[...], value_ref[...])
    row = lax.broadcasted_iota(jnp.int32, (size, size), 0)
    col = lax.broadcasted_iota(jnp.int32, (size, size), 1)
    reverse = jnp.where(row + col == size - 1, 1.0, 0.0).astype(BF16)
    flipped = [
        matmul(reverse, opposite_ref[(n - 1 - i) * size : (n - i) * size]).astype(BF16) for i in range(n)
    ]
    mirrored = matmul(jnp.concatenate(flipped, 0), gate_ref[...]).astype(BF16)
    gated = (value * jax.nn.sigmoid(mirrored.astype(F32))).astype(BF16)
    result[...] = matmul(gated, out_ref[...]).astype(BF16)
    for k, out in enumerate(outs):
        at = lax.rem(j + k, n)
        out[...] = result[pl.ds(pl.multiple_of(at * size, size), size)]


def local_spread(
    seq_in, conv_norm, conv_weight, ff_norm, up_weight, down_weight,
    head_norm, value_weight, gate_weight, out_weight,
):
    n = lax.axis_size("seq")
    blocks, taps, width, chans = conv_weight.shape
    hidden = up_weight.shape[2]
    half = hidden // 2
    rows = seq_in.shape[1]
    part = jax.ShapeDtypeStruct((rows // n, width), BF16)
    turned = jnp.swapaxes(conv_weight, 2, 3)
    cut = hidden + taps * chans
    shard = (up_weight, down_weight, turned, turned, up_weight, down_weight)
    which = (0, 0, 0, 1, 1, 1), (True, False, False, False, True, False)
    own = pack(shard, *which, cut + hidden, True)
    to = lambda k: (lambda g, i, s, c: (g, (i + k) % n, s, c if s == 0 else 1 - c))
    parts = pl.pallas_call(
        split_kernel, out_shape=[part] * n, in_specs=[VMEM_SPEC], out_specs=[VMEM_SPEC] * n,
        compiler_params=PARAMS, name="split",
    )(seq_in[0])

    a = along(own)
    x = across(own)
    b = along(a)
    xa = across(a)
    ya = planes(a)
    swaps = [other_core(a), other_core(x)]
    states = [moved(parts[0], to(0))]
    events = [*swaps, states[0]]
    parts = after(parts, [b, ya, *events])
    size = cut + hidden
    yxa = planes(xa)
    keep = size - 176
    xb0 = across(b[:keep])
    xb1 = along(xa[keep:])
    states += [moved(p, to(k + 1)) for k, p in enumerate(parts[1:])]
    xb = jnp.concatenate([xb0, xb1], 0)
    rest = pack(shard, *which, cut + hidden, False)
    mine = [own, a, b, x, xa, xb, ya, yxa]
    swap_a, swap_x = swaps
    bs, xas, yas = after([b, xa, ya], [states[-1]])
    others = [swap_a, other_core(bs), swap_x, other_core(xas), other_core(xb), other_core(yas), other_core(yxa)]
    arrays = mine + [rest] + others
    places = [[(k, 0) for k in range(8)], [(k + 8, 0) for k in range(8)]]
    head = head_norm[None]
    state = conv(states, conv_norm, arrays, places, 0, hidden, taps)
    (state,) = feed_forward(state, None, ff_norm, head, arrays, places, 0, 0, half, "state")
    state = conv([state], conv_norm, arrays, places, 1, hidden + taps * chans // 2, taps)
    (final,) = feed_forward(state, None, ff_norm, head, arrays, places, 1, cut, half, "head")
    opposite = other_core(final)
    results = pl.pallas_call(
        head_kernel, out_shape=[part] * n, in_specs=[VMEM_SPEC] * 5, out_specs=[VMEM_SPEC] * n,
        scratch_shapes=[pltpu.VMEM((rows, width), BF16)], compiler_params=PARAMS, name="head",
    )(final, opposite, value_weight, gate_weight, out_weight)
    home = [moved(r, to(k)) for k, r in enumerate(results)]
    joined = pl.pallas_call(
        join_kernel, out_shape=jax.ShapeDtypeStruct((rows, width), BF16), in_specs=[VMEM_SPEC] * n,
        out_specs=VMEM_SPEC, compiler_params=PARAMS, name="join",
    )(*home)
    return joined[None]


def solution(mesh):
    in_specs = (
        P("strand", ("groups", "seq", "chan"), None),
        P(),
        P(None, None, None, ("seq", "chan")),
        P(),
        P(None, None, ("seq", "chan")),
        P(None, ("seq", "chan"), None),
        P(),
        P(),
        P(),
        P(),
    )
    out_specs = P("strand", ("groups", "seq", "chan"), None)

    def step(seq_in, conv_norm, conv_weight, *rest):
        size = mesh.shape
        shards = size["seq"] * size["chan"]
        tiled = conv_weight.shape[3] % (32 * shards) == 0
        blocks = conv_weight.shape[0]
        spread = tiled and blocks == 2 and [size[a] for a in AXES] == [2, 4, 2, 2]
        local = local_spread if spread else local_plain
        run = jax.shard_map(local, mesh=mesh, in_specs=in_specs, out_specs=out_specs, check_vma=False)
        return run(seq_in, conv_norm, conv_weight, *rest)

    return step
```

```python
import functools
import itertools

import jax
import jax.numpy as jnp
from jax import lax
from jax.experimental import pallas as pl
from jax.experimental.pallas import tpu as pltpu
from jax.sharding import PartitionSpec as P

AXES = ("groups", "seq", "strand", "chan")
BF16, F32 = jnp.bfloat16, jnp.float32
PARAMS = pltpu.CompilerParams(vmem_limit_bytes=40 * 2**20)
VMEM_SPEC = pl.BlockSpec(memory_space=pltpu.VMEM)


def normalize(values, gain):
    return values * lax.rsqrt(jnp.mean(values * values, axis=-1, keepdims=True) + 1e-06) * gain


def matmul(left, right):
    return jnp.dot(left, right, preferred_element_type=F32)


def matmul_nt(left, right):
    return lax.dot_general(left, right, (((1,), (1,)), ((), ())), preferred_element_type=F32)


def passed_along(value, axis, steps):
    count = lax.axis_size(axis)
    initial, last = (max(0, -steps), min(count, count - steps))
    return lax.ppermute(value, axis, [(source, source + steps) for source in range(initial, last)])


def swapped(x, axis, stride):
    return lax.ppermute(x, axis, [(i, i ^ 1 << stride) for i in range(lax.axis_size(axis))])


def local_plain(
    seq_in, conv_norm, conv_weight, ff_norm, up_weight, down_weight,
    head_norm, value_weight, gate_weight, out_weight,
):
    state = seq_in[0].astype(F32)
    seq_count = lax.axis_size("seq")
    for block in range(conv_weight.shape[0]):
        reach = min(2**block, seq_count // 2)
        normed = normalize(state, conv_norm[block]).astype(BF16)
        before = passed_along(normed, "seq", reach)
        after = passed_along(normed, "seq", -reach)
        piece = lax.all_gather(conv_weight[block], ("seq", "chan"), axis=2, tiled=True)
        total = matmul(before, piece[0]) + matmul(normed, piece[1]) + matmul(after, piece[2])
        state = state + total.astype(BF16).astype(F32)
        mixed = normalize(state, ff_norm[block]).astype(BF16)
        up = lax.all_gather(up_weight[block], ("seq", "chan"), axis=1, tiled=True)
        hidden = jax.nn.gelu(matmul(mixed, up)).astype(BF16)
        down = lax.all_gather(down_weight[block], ("seq", "chan"), axis=0, tiled=True)
        state = state + matmul(hidden, down)
    final = normalize(state, head_norm).astype(BF16)
    value = matmul(final, value_weight)
    bit_count = (seq_count * lax.axis_size("chan")).bit_length() - 1
    opposite = swapped(final, "strand", 0)
    for digit in range(bit_count):
        opposite = swapped(opposite, ("seq", "chan"), digit)
    opposite = jnp.flip(opposite, 0)
    mirrored = matmul(opposite, gate_weight).astype(BF16)
    gated = (value * jax.nn.sigmoid(mirrored.astype(F32))).astype(BF16)
    return matmul(gated, out_weight).astype(BF16)[None]


def moved(value, go):
    sizes = [lax.axis_size(a) for a in AXES]

    def flat(at):
        number = 0
        for n, k in zip(sizes, at):
            number = number * n + k
        return number

    pairs = [(flat(at), flat(go(*at))) for at in itertools.product(*map(range, sizes))]
    return lax.ppermute(value, AXES, pairs)


def across(value):
    return moved(value, lambda g, i, s, c: (g, i, s, 1 - c))


def planes(value):
    return moved(value, lambda g, i, s, c: (1 - g, i, s, c))


def other_core(value):
    return moved(value, lambda g, i, s, c: (g, i, 1 - s, c))


def along(value):
    n = lax.axis_size("seq")
    return moved(value, lambda g, i, s, c: (g, (i + 1 - 2 * g) % n, s, c))


def after(values, events):
    values, _ = lax.optimization_barrier((tuple(values), tuple(events)))
    return values


def origins():
    g, i, c = (lax.axis_index(a) for a in ("groups", "seq", "chan"))
    n, m = lax.axis_size("seq"), lax.axis_size("chan")
    a = lax.rem(i + n - 1 + 2 * g, n)
    b = lax.rem(i + 2, n)
    ya = lax.rem(i + n + 1 - 2 * g, n)
    x = 1 - c
    at = [(i, c), (a, c), (b, c), (i, x), (a, x), (b, x), (ya, c), (ya, x)]
    return [k * m + h for k, h in at]


def pack_kernel(plan, mine, *refs):
    blocks, turned = plan
    refs, (out, wide, sems) = refs[:-3], refs[-3:]
    s = lax.axis_index("strand")
    part = s if mine else 1 - s
    at, turns, copies = 0, [], []

    def copy(source, target):
        copies.append(pltpu.make_async_copy(source, target, sems.at[len(copies)]))
        copies[-1].start()

    for ref, block, turn in zip(refs, blocks, turned):
        if turn:
            half = ref.shape[2] // 2
            columns = pl.ds(pl.multiple_of(part * half, half), half)
            copy(ref.at[block, :, columns], wide.at[len(turns)])
            turns.append((at, half, copies[-1]))
            at += half
        else:
            half = ref.shape[-2] // 2
            rows = pl.ds(pl.multiple_of(part * half, half), half)
            for tap in range(ref.shape[1]) if len(ref.shape) == 4 else (None,):
                source = ref.at[block, rows] if tap is None else ref.at[block, tap, rows]
                copy(source, out.at[at : at + half])
                at += half
    for k, (at, half, done) in enumerate(turns):
        done.wait()
        out[at : at + half] = wide[k].T
    for done in copies:
        if all(done is not turn[2] for turn in turns):
            done.wait()


def pack(arrays, blocks, turned, rows, mine):
    width = arrays[0].shape[1]
    half = arrays[0].shape[2] // 2
    return pl.pallas_call(
        functools.partial(pack_kernel, (blocks, turned), mine),
        out_shape=jax.ShapeDtypeStruct((rows, width), BF16),
        in_specs=[pl.BlockSpec(memory_space=pltpu.HBM)] * len(arrays),
        out_specs=VMEM_SPEC,
        scratch_shapes=[
            pltpu.VMEM((sum(turned), width, half), BF16),
            pltpu.SemaphoreType.DMA((2 * rows // 32,)),
        ],
        compiler_params=PARAMS,
        name="pack_own" if mine else "pack_rest",
    )(*[pltpu.with_memory_space_constraint(v, pltpu.HBM) for v in arrays])


def split_kernel(rows_ref, *out_refs):
    n = lax.axis_size("seq")
    i, s = lax.axis_index("seq"), lax.axis_index("strand")
    size = out_refs[0].shape[0]
    for k, out in enumerate(out_refs):
        j = i ^ k
        sub = jnp.where(s == 0, j, n - 1 - j)
        out[...] = rows_ref[pl.ds(pl.multiple_of(sub * size, size), size)]


def join_kernel(*refs):
    *parts, out = refs
    n = lax.axis_size("seq")
    i, s = lax.axis_index("seq"), lax.axis_index("strand")
    size = parts[0].shape[0]
    for k, part in enumerate(parts):
        j = i ^ k
        sub = jnp.where(s == 0, j, n - 1 - j)
        out[pl.ds(pl.multiple_of(sub * size, size), size)] = part[...]


def conv_kernel(block, parts, places, start, gain_ref, *refs):
    n = lax.axis_size("seq")
    states, arrays = refs[:parts], refs[parts:-3]
    out, weight, acc = refs[-3:]
    width = acc.shape[1]
    taps = weight.shape[0] // width
    half = width // len(places[0]) // 2
    s, j = lax.axis_index("strand"), lax.axis_index("seq")
    for side, part in zip(places, (s, 1 - s)):
        for (k, row), shard in zip(side, origins()):
            at = pl.multiple_of((shard * 2 + part) * half, half)
            for tap in range(taps):
                first = row + start + tap * half
                weight[pl.ds(tap * width + at, half)] = arrays[k][first : first + half]
    if parts > 1:
        size = states[0].shape[0]
        for k, state in enumerate(states):
            at = j ^ k
            out[pl.ds(pl.multiple_of(at * size, size), size)] = state[...].astype(F32)
        state = out[...]
    else:
        state = states[0][...]
    normed = normalize(state, gain_ref[block : block + 1]).astype(BF16)
    shift = state.shape[0] // n * min(2**block, n // 2)
    acc[...] = matmul_nt(normed, weight[width : 2 * width])
    acc[shift:] += matmul_nt(normed[:-shift], weight[:width])
    acc[:-shift] += matmul_nt(normed[shift:], weight[2 * width :])
    out[...] = state + acc[...].astype(BF16).astype(F32)


def conv(states, gain, arrays, places, block, start, taps):
    width = gain.shape[1]
    rows = sum(v.shape[0] for v in states)
    return pl.pallas_call(
        functools.partial(conv_kernel, block, len(states), places, start),
        out_shape=jax.ShapeDtypeStruct((rows, width), F32),
        in_specs=[VMEM_SPEC] * (1 + len(states) + len(arrays)),
        out_specs=VMEM_SPEC,
        scratch_shapes=[pltpu.VMEM((taps * width, width), BF16), pltpu.VMEM((rows, width), F32)],
        compiler_params=PARAMS,
        name=f"conv{block}",
    )(gain, *states, *arrays)


def ff_kernel(block, first, ends, places, start, half, gain_ref, head_ref, state_ref, *refs):
    if not first:
        mixed_ref, refs = refs[0], refs[1:]
    arrays, out, hid = refs, refs[-2 if ends else -3], refs[-1]
    state = state_ref[...]
    if first:
        mixed = normalize(state, gain_ref[block : block + 1]).astype(BF16)
    else:
        mixed = mixed_ref[...]
    down = []
    for r, pair in enumerate(zip(*places)):
        up = jnp.concatenate([arrays[k][row + start : row + start + half] for k, row in pair], 0)
        hid[:, 2 * r * half : 2 * (r + 1) * half] = jax.nn.gelu(matmul_nt(mixed, up)).astype(BF16)
        down += [arrays[k][row + start + half : row + start + 2 * half] for k, row in pair]
    state = state + matmul(hid[...], jnp.concatenate(down, 0))
    if ends == "head":
        state = normalize(state, head_ref[...]).astype(BF16)
    out[...] = state
    if not ends:
        refs[-2][...] = mixed


def feed_forward(state, mixed, gain, head, arrays, places, block, start, half, ends):
    rows, width = state.shape
    out = [jax.ShapeDtypeStruct((rows, width), BF16 if ends == "head" else F32)]
    if not ends:
        out.append(jax.ShapeDtypeStruct((rows, width), BF16))
    given = [state] if mixed is None else [state, mixed]
    return pl.pallas_call(
        functools.partial(ff_kernel, block, mixed is None, ends, places, start, half),
        out_shape=out,
        in_specs=[VMEM_SPEC] * (2 + len(given) + len(arrays)),
        out_specs=[VMEM_SPEC] * len(out),
        scratch_shapes=[pltpu.VMEM((rows, 2 * len(places[0]) * half), BF16)],
        compiler_params=PARAMS,
        name=f"ff{block}",
    )(gain, head, *given, *arrays)


def head_kernel(final_ref, opposite_ref, value_ref, gate_ref, out_ref, *refs):
    *outs, result = refs
    n = len(outs)
    size = outs[0].shape[0]
    j = lax.axis_index("seq")
    value = matmul(final_ref[...], value_ref[...])
    row = lax.broadcasted_iota(jnp.int32, (size, size), 0)
    col = lax.broadcasted_iota(jnp.int32, (size, size), 1)
    reverse = jnp.where(row + col == size - 1, 1.0, 0.0).astype(BF16)
    flipped = [
        matmul(reverse, opposite_ref[(n - 1 - i) * size : (n - i) * size]).astype(BF16) for i in range(n)
    ]
    mirrored = matmul(jnp.concatenate(flipped, 0), gate_ref[...]).astype(BF16)
    gated = (value * jax.nn.sigmoid(mirrored.astype(F32))).astype(BF16)
    result[...] = matmul(gated, out_ref[...]).astype(BF16)
    for k, out in enumerate(outs):
        at = j ^ k
        out[...] = result[pl.ds(pl.multiple_of(at * size, size), size)]


def local_spread(
    seq_in, conv_norm, conv_weight, ff_norm, up_weight, down_weight,
    head_norm, value_weight, gate_weight, out_weight,
):
    n = lax.axis_size("seq")
    blocks, taps, width, chans = conv_weight.shape
    hidden = up_weight.shape[2]
    half = hidden // 2
    rows = seq_in.shape[1]
    part = jax.ShapeDtypeStruct((rows // n, width), BF16)
    turned = jnp.swapaxes(conv_weight, 2, 3)
    cut = hidden + taps * chans
    shard = (up_weight, down_weight, turned, turned, up_weight, down_weight)
    which = (0, 0, 0, 1, 1, 1), (True, False, False, False, True, False)
    own = pack(shard, *which, cut + hidden, True)
    to = lambda k: (lambda g, i, s, c: (g, i ^ k, s, c if s == 0 else 1 - c))
    parts = pl.pallas_call(
        split_kernel, out_shape=[part] * n, in_specs=[VMEM_SPEC], out_specs=[VMEM_SPEC] * n,
        compiler_params=PARAMS, name="split",
    )(seq_in[0])

    a = along(own)
    x = across(own)
    b = along(a)
    xa = across(a)
    ya = planes(a)
    swaps = [other_core(a), other_core(x)]
    states = [moved(parts[0], to(0))]
    first = after(shard[:3], [x])
    rest = pack((*first[:3], first[2], *first[:2]), *which, cut + hidden, False)
    b, xa, ya, rest, swaps[0], swaps[1], states[0], *parts = after(
        [b, xa, ya, rest, *swaps, states[0], *parts[1:]], []
    )
    yxa0 = planes(xa[:cut])
    xb0 = across(b[:cut])
    states += [moved(p, to(k + 1)) for k, p in enumerate(parts)]
    bl, xal, yal, xb0, yxa0, *states = after([b, xa, ya, xb0, yxa0, *states], [])
    sxb0, syxa0 = other_core(xb0), other_core(yxa0)
    (bs,) = after([bl], [sxb0])
    xas, yas = after([xal, yal], [syxa0])
    sb, sxa, sya = other_core(bs), other_core(xas), other_core(yas)
    yxa1 = planes(xal[cut:])
    xb1 = across(bl[cut:])
    mine = [own, a, b, x, xa, ya]
    others = [rest, swaps[0], sb, swaps[1], sxa, sya]
    arrays = mine + [xb0, yxa0] + others + [sxb0, syxa0]
    places = [
        [(k, 0) for k in (0, 1, 2, 3, 4, 6, 5, 7)],
        [(8, 0), (9, 0), (10, 0), (11, 0), (12, 0), (14, 0), (13, 0), (15, 0)],
    ]
    early = [[(k, 0) for k in range(6)], [(k + 6, 0) for k in range(6)]]
    head = head_norm[None]
    state = conv0 = conv(states, conv_norm, arrays, places, 0, hidden, taps)
    (state,) = (ff0,) = feed_forward(state, None, ff_norm, head, arrays, places, 0, 0, half, "state")
    state = conv1 = conv([state], conv_norm, arrays, places, 1, hidden + taps * chans // 2, taps)
    state, mixed = feed_forward(state, None, ff_norm, head, mine + others, early, 1, cut, half, "")
    late = jnp.concatenate(after([xb1, yxa1], [conv1]), 0)
    places = [[(0, 0), (0, hidden)], [(1, 0), (1, hidden)]]
    arrays = [late, other_core(late)]
    (final,) = feed_forward(state, mixed, ff_norm, head, arrays, places, 1, 0, half, "head")
    opposite = other_core(final)
    results = pl.pallas_call(
        head_kernel, out_shape=[part] * n, in_specs=[VMEM_SPEC] * 5, out_specs=[VMEM_SPEC] * n,
        scratch_shapes=[pltpu.VMEM((rows, width), BF16)], compiler_params=PARAMS, name="head",
    )(final, opposite, value_weight, gate_weight, out_weight)
    home = {k: moved(results[k], to(k)) for k in (2, 3, 1, 0)}
    home = [home[k] for k in range(n)]
    joined = pl.pallas_call(
        join_kernel, out_shape=jax.ShapeDtypeStruct((rows, width), BF16), in_specs=[VMEM_SPEC] * n,
        out_specs=VMEM_SPEC, compiler_params=PARAMS, name="join",
    )(*home)
    return joined[None]


def solution(mesh):
    in_specs = (
        P("strand", ("groups", "seq", "chan"), None),
        P(),
        P(None, None, None, ("seq", "chan")),
        P(),
        P(None, None, ("seq", "chan")),
        P(None, ("seq", "chan"), None),
        P(),
        P(),
        P(),
        P(),
    )
    out_specs = P("strand", ("groups", "seq", "chan"), None)

    def step(seq_in, conv_norm, conv_weight, *rest):
        size = mesh.shape
        shards = size["seq"] * size["chan"]
        tiled = conv_weight.shape[3] % (32 * shards) == 0
        blocks = conv_weight.shape[0]
        spread = tiled and blocks == 2 and [size[a] for a in AXES] == [2, 4, 2, 2]
        local = local_spread if spread else local_plain
        run = jax.shard_map(local, mesh=mesh, in_specs=in_specs, out_specs=out_specs, check_vma=False)
        return run(seq_in, conv_norm, conv_weight, *rest)

    return step
```

```python
import functools
import itertools

import jax
import jax.numpy as jnp
from jax import lax
from jax.experimental import pallas as pl
from jax.experimental.pallas import tpu as pltpu
from jax.sharding import PartitionSpec as P

AXES = ("groups", "seq", "strand", "chan")
BF16, F32 = jnp.bfloat16, jnp.float32
PARAMS = pltpu.CompilerParams(vmem_limit_bytes=40 * 2**20)
VMEM_SPEC = pl.BlockSpec(memory_space=pltpu.VMEM)


def normalize(values, gain):
    return values * lax.rsqrt(jnp.mean(values * values, axis=-1, keepdims=True) + 1e-06) * gain


def matmul(left, right):
    return jnp.dot(left, right, preferred_element_type=F32)


def matmul_nt(left, right):
    return lax.dot_general(left, right, (((1,), (1,)), ((), ())), preferred_element_type=F32)


def passed_along(value, axis, steps):
    count = lax.axis_size(axis)
    initial, last = (max(0, -steps), min(count, count - steps))
    return lax.ppermute(value, axis, [(source, source + steps) for source in range(initial, last)])


def swapped(x, axis, stride):
    return lax.ppermute(x, axis, [(i, i ^ 1 << stride) for i in range(lax.axis_size(axis))])


def local_plain(
    seq_in, conv_norm, conv_weight, ff_norm, up_weight, down_weight,
    head_norm, value_weight, gate_weight, out_weight,
):
    state = seq_in[0].astype(F32)
    seq_count = lax.axis_size("seq")
    for block in range(conv_weight.shape[0]):
        reach = min(2**block, seq_count // 2)
        normed = normalize(state, conv_norm[block]).astype(BF16)
        before = passed_along(normed, "seq", reach)
        after = passed_along(normed, "seq", -reach)
        piece = lax.all_gather(conv_weight[block], ("seq", "chan"), axis=2, tiled=True)
        total = matmul(before, piece[0]) + matmul(normed, piece[1]) + matmul(after, piece[2])
        state = state + total.astype(BF16).astype(F32)
        mixed = normalize(state, ff_norm[block]).astype(BF16)
        up = lax.all_gather(up_weight[block], ("seq", "chan"), axis=1, tiled=True)
        hidden = jax.nn.gelu(matmul(mixed, up)).astype(BF16)
        down = lax.all_gather(down_weight[block], ("seq", "chan"), axis=0, tiled=True)
        state = state + matmul(hidden, down)
    final = normalize(state, head_norm).astype(BF16)
    value = matmul(final, value_weight)
    bit_count = (seq_count * lax.axis_size("chan")).bit_length() - 1
    opposite = swapped(final, "strand", 0)
    for digit in range(bit_count):
        opposite = swapped(opposite, ("seq", "chan"), digit)
    opposite = jnp.flip(opposite, 0)
    mirrored = matmul(opposite, gate_weight).astype(BF16)
    gated = (value * jax.nn.sigmoid(mirrored.astype(F32))).astype(BF16)
    return matmul(gated, out_weight).astype(BF16)[None]


def moved(value, go):
    sizes = [lax.axis_size(a) for a in AXES]

    def flat(at):
        number = 0
        for n, k in zip(sizes, at):
            number = number * n + k
        return number

    pairs = [(flat(at), flat(go(*at))) for at in itertools.product(*map(range, sizes))]
    return lax.ppermute(value, AXES, pairs)


def across(value):
    return moved(value, lambda g, i, s, c: (g, i, s, 1 - c))


def planes(value):
    return moved(value, lambda g, i, s, c: (1 - g, i, s, c))


def other_core(value):
    return moved(value, lambda g, i, s, c: (g, i, 1 - s, c))


def along(value):
    n = lax.axis_size("seq")
    return moved(value, lambda g, i, s, c: (g, (i + 1 - 2 * g) % n, s, c))


def after(values, events):
    values, _ = lax.optimization_barrier((tuple(values), tuple(events)))
    return values


def origins():
    g, i, c = (lax.axis_index(a) for a in ("groups", "seq", "chan"))
    n, m = lax.axis_size("seq"), lax.axis_size("chan")
    a = lax.rem(i + n - 1 + 2 * g, n)
    b = lax.rem(i + 2, n)
    ya = lax.rem(i + n + 1 - 2 * g, n)
    x = 1 - c
    at = [(i, c), (a, c), (b, c), (i, x), (a, x), (b, x), (ya, c), (ya, x)]
    return [k * m + h for k, h in at]


def pack_kernel(plan, mine, *refs):
    blocks, turned = plan
    refs, (out, wide, sems) = refs[:-3], refs[-3:]
    s = lax.axis_index("strand")
    part = s if mine else 1 - s
    at, turns, copies = 0, [], []

    def copy(source, target):
        copies.append(pltpu.make_async_copy(source, target, sems.at[len(copies)]))
        copies[-1].start()

    for ref, block, turn in zip(refs, blocks, turned):
        if turn:
            half = ref.shape[2] // 2
            columns = pl.ds(pl.multiple_of(part * half, half), half)
            copy(ref.at[block, :, columns], wide.at[len(turns)])
            turns.append((at, half, copies[-1]))
            at += half
        else:
            half = ref.shape[-2] // 2
            rows = pl.ds(pl.multiple_of(part * half, half), half)
            for tap in range(ref.shape[1]) if len(ref.shape) == 4 else (None,):
                source = ref.at[block, rows] if tap is None else ref.at[block, tap, rows]
                copy(source, out.at[at : at + half])
                at += half
    for k, (at, half, done) in enumerate(turns):
        done.wait()
        out[at : at + half] = wide[k].T
    for done in copies:
        if all(done is not turn[2] for turn in turns):
            done.wait()


def pack(arrays, blocks, turned, rows, mine):
    width = arrays[0].shape[1]
    half = arrays[0].shape[2] // 2
    return pl.pallas_call(
        functools.partial(pack_kernel, (blocks, turned), mine),
        out_shape=jax.ShapeDtypeStruct((rows, width), BF16),
        in_specs=[pl.BlockSpec(memory_space=pltpu.HBM)] * len(arrays),
        out_specs=VMEM_SPEC,
        scratch_shapes=[
            pltpu.VMEM((sum(turned), width, half), BF16),
            pltpu.SemaphoreType.DMA((2 * rows // 32,)),
        ],
        compiler_params=PARAMS,
        name="pack_own" if mine else "pack_rest",
    )(*[pltpu.with_memory_space_constraint(v, pltpu.HBM) for v in arrays])


def split_kernel(rows_ref, *out_refs):
    n = lax.axis_size("seq")
    i, s = lax.axis_index("seq"), lax.axis_index("strand")
    size = out_refs[0].shape[0]
    for k, out in enumerate(out_refs):
        j = i ^ k
        sub = jnp.where(s == 0, j, n - 1 - j)
        out[...] = rows_ref[pl.ds(pl.multiple_of(sub * size, size), size)]


def join_kernel(*refs):
    *parts, out = refs
    n = lax.axis_size("seq")
    i, s = lax.axis_index("seq"), lax.axis_index("strand")
    size = parts[0].shape[0]
    for k, part in enumerate(parts):
        j = i ^ k
        sub = jnp.where(s == 0, j, n - 1 - j)
        out[pl.ds(pl.multiple_of(sub * size, size), size)] = part[...]


def conv_kernel(block, parts, places, start, gain_ref, *refs):
    n = lax.axis_size("seq")
    states, arrays = refs[:parts], refs[parts:-3]
    out, weight, acc = refs[-3:]
    width = acc.shape[1]
    taps = weight.shape[0] // width
    half = width // len(places[0]) // 2
    s, j = lax.axis_index("strand"), lax.axis_index("seq")
    for side, part in zip(places, (s, 1 - s)):
        for (k, row), shard in zip(side, origins()):
            at = pl.multiple_of((shard * 2 + part) * half, half)
            for tap in range(taps):
                first = row + start + tap * half
                weight[pl.ds(tap * width + at, half)] = arrays[k][first : first + half]
    if parts > 1:
        size = states[0].shape[0]
        for k, state in enumerate(states):
            at = j ^ k
            out[pl.ds(pl.multiple_of(at * size, size), size)] = state[...].astype(F32)
        state = out[...]
    else:
        state = states[0][...]
    normed = normalize(state, gain_ref[block : block + 1]).astype(BF16)
    shift = state.shape[0] // n * min(2**block, n // 2)
    acc[...] = matmul_nt(normed, weight[width : 2 * width])
    acc[shift:] += matmul_nt(normed[:-shift], weight[:width])
    acc[:-shift] += matmul_nt(normed[shift:], weight[2 * width :])
    out[...] = state + acc[...].astype(BF16).astype(F32)


def conv(states, gain, arrays, places, block, start, taps):
    width = gain.shape[1]
    rows = sum(v.shape[0] for v in states)
    return pl.pallas_call(
        functools.partial(conv_kernel, block, len(states), places, start),
        out_shape=jax.ShapeDtypeStruct((rows, width), F32),
        in_specs=[VMEM_SPEC] * (1 + len(states) + len(arrays)),
        out_specs=VMEM_SPEC,
        scratch_shapes=[pltpu.VMEM((taps * width, width), BF16), pltpu.VMEM((rows, width), F32)],
        compiler_params=PARAMS,
        name=f"conv{block}",
    )(gain, *states, *arrays)


def ff_kernel(block, first, ends, places, start, half, gain_ref, head_ref, state_ref, *refs):
    if not first:
        mixed_ref, refs = refs[0], refs[1:]
    arrays, out, hid = refs, refs[-2 if ends else -3], refs[-1]
    state = state_ref[...]
    if first:
        mixed = normalize(state, gain_ref[block : block + 1]).astype(BF16)
    else:
        mixed = mixed_ref[...]
    down = []
    for r, pair in enumerate(zip(*places)):
        up = jnp.concatenate([arrays[k][row + start : row + start + half] for k, row in pair], 0)
        hid[:, 2 * r * half : 2 * (r + 1) * half] = jax.nn.gelu(matmul_nt(mixed, up)).astype(BF16)
        down += [arrays[k][row + start + half : row + start + 2 * half] for k, row in pair]
    state = state + matmul(hid[...], jnp.concatenate(down, 0))
    if ends == "head":
        state = normalize(state, head_ref[...]).astype(BF16)
    out[...] = state
    if not ends:
        refs[-2][...] = mixed


def feed_forward(state, mixed, gain, head, arrays, places, block, start, half, ends):
    rows, width = state.shape
    out = [jax.ShapeDtypeStruct((rows, width), BF16 if ends == "head" else F32)]
    if not ends:
        out.append(jax.ShapeDtypeStruct((rows, width), BF16))
    given = [state] if mixed is None else [state, mixed]
    return pl.pallas_call(
        functools.partial(ff_kernel, block, mixed is None, ends, places, start, half),
        out_shape=out,
        in_specs=[VMEM_SPEC] * (2 + len(given) + len(arrays)),
        out_specs=[VMEM_SPEC] * len(out),
        scratch_shapes=[pltpu.VMEM((rows, 2 * len(places[0]) * half), BF16)],
        compiler_params=PARAMS,
        name=f"ff{block}",
    )(gain, head, *given, *arrays)


def head_kernel(final_ref, opposite_ref, value_ref, gate_ref, out_ref, *refs):
    *outs, result = refs
    n = len(outs)
    size = outs[0].shape[0]
    j = lax.axis_index("seq")
    value = matmul(final_ref[...], value_ref[...])
    row = lax.broadcasted_iota(jnp.int32, (size, size), 0)
    col = lax.broadcasted_iota(jnp.int32, (size, size), 1)
    reverse = jnp.where(row + col == size - 1, 1.0, 0.0).astype(BF16)
    flipped = [
        matmul(reverse, opposite_ref[(n - 1 - i) * size : (n - i) * size]).astype(BF16) for i in range(n)
    ]
    mirrored = matmul(jnp.concatenate(flipped, 0), gate_ref[...]).astype(BF16)
    gated = (value * jax.nn.sigmoid(mirrored.astype(F32))).astype(BF16)
    result[...] = matmul(gated, out_ref[...]).astype(BF16)
    for k, out in enumerate(outs):
        at = j ^ k
        out[...] = result[pl.ds(pl.multiple_of(at * size, size), size)]


def local_spread(
    seq_in, conv_norm, conv_weight, ff_norm, up_weight, down_weight,
    head_norm, value_weight, gate_weight, out_weight,
):
    n = lax.axis_size("seq")
    blocks, taps, width, chans = conv_weight.shape
    hidden = up_weight.shape[2]
    half = hidden // 2
    rows = seq_in.shape[1]
    part = jax.ShapeDtypeStruct((rows // n, width), BF16)
    turned = jnp.swapaxes(conv_weight, 2, 3)
    cut = hidden + taps * chans
    shard = (up_weight, down_weight, turned, turned, up_weight, down_weight)
    which = (0, 0, 0, 1, 1, 1), (True, False, False, False, True, False)
    own = pack(shard, *which, cut + hidden, True)
    to = lambda k: (lambda g, i, s, c: (g, i ^ k, s, c if s == 0 else 1 - c))
    parts = pl.pallas_call(
        split_kernel, out_shape=[part] * n, in_specs=[VMEM_SPEC], out_specs=[VMEM_SPEC] * n,
        compiler_params=PARAMS, name="split",
    )(seq_in[0])

    a = along(own)
    x = across(own)
    b = along(a)
    xa = across(a)
    ya = planes(a)
    swaps = [other_core(a), other_core(x)]
    states = [moved(parts[0], to(0))]
    first = after(shard[:3], [x])
    rest = pack((*first[:3], first[2], *first[:2]), *which, cut + hidden, False)
    b, xa, ya, rest, swaps[0], swaps[1], states[0], *parts = after(
        [b, xa, ya, rest, *swaps, states[0], *parts[1:]], []
    )
    yxa0 = planes(xa[:cut])
    xb0 = across(b[:cut])
    states += [moved(p, to(k + 1)) for k, p in enumerate(parts)]
    bl, xal, yal, xb0, yxa0, *states = after([b, xa, ya, xb0, yxa0, *states], [])
    stay = [bl, xal, yal]
    swap0 = other_core(jnp.concatenate([*(v[:cut] for v in stay), xb0, yxa0], 0))
    yxa1 = planes(xal[cut:])
    xb1 = across(bl[cut:])
    mine = [own, a, b, x, xa, ya]
    others = [rest, *swaps]
    arrays = mine + [xb0, yxa0] + others + [swap0]
    places = [
        [(k, 0) for k in (0, 1, 2, 3, 4, 6, 5, 7)],
        [(8, 0), (9, 0), (11, 0), (10, 0), (11, cut), (11, 3 * cut), (11, 2 * cut), (11, 4 * cut)],
    ]
    early = [
        [(k, cut) for k in range(6)],
        [(6, cut), (7, cut), (9, 0), (8, cut), (9, hidden), (9, 2 * hidden)],
    ]
    head = head_norm[None]
    state = conv0 = conv(states, conv_norm, arrays, places, 0, hidden, taps)
    (state,) = (ff0,) = feed_forward(state, None, ff_norm, head, arrays, places, 0, 0, half, "state")
    state = conv1 = conv([state], conv_norm, arrays, places, 1, hidden + taps * chans // 2, taps)
    tail, _ = lax.optimization_barrier((jnp.concatenate([v[cut:] for v in stay], 0), conv0))
    swap1 = other_core(tail)
    state, mixed = feed_forward(
        state, None, ff_norm, head, mine + others + [swap1], early, 1, 0, half, ""
    )
    late = jnp.concatenate(after([xb1, yxa1], [conv1]), 0)
    places = [[(0, 0), (0, hidden)], [(1, 0), (1, hidden)]]
    arrays = [late, other_core(late)]
    (final,) = feed_forward(state, mixed, ff_norm, head, arrays, places, 1, 0, half, "head")
    opposite = other_core(final)
    results = pl.pallas_call(
        head_kernel, out_shape=[part] * n, in_specs=[VMEM_SPEC] * 5, out_specs=[VMEM_SPEC] * n,
        scratch_shapes=[pltpu.VMEM((rows, width), BF16)], compiler_params=PARAMS, name="head",
    )(final, opposite, value_weight, gate_weight, out_weight)
    home = {k: moved(results[k], to(k)) for k in (2, 3, 1, 0)}
    home = [home[k] for k in range(n)]
    joined = pl.pallas_call(
        join_kernel, out_shape=jax.ShapeDtypeStruct((rows, width), BF16), in_specs=[VMEM_SPEC] * n,
        out_specs=VMEM_SPEC, compiler_params=PARAMS, name="join",
    )(*home)
    return joined[None]


def solution(mesh):
    in_specs = (
        P("strand", ("groups", "seq", "chan"), None),
        P(),
        P(None, None, None, ("seq", "chan")),
        P(),
        P(None, None, ("seq", "chan")),
        P(None, ("seq", "chan"), None),
        P(),
        P(),
        P(),
        P(),
    )
    out_specs = P("strand", ("groups", "seq", "chan"), None)

    def step(seq_in, conv_norm, conv_weight, *rest):
        size = mesh.shape
        shards = size["seq"] * size["chan"]
        tiled = conv_weight.shape[3] % (32 * shards) == 0
        blocks = conv_weight.shape[0]
        spread = tiled and blocks == 2 and [size[a] for a in AXES] == [2, 4, 2, 2]
        local = local_spread if spread else local_plain
        run = jax.shard_map(local, mesh=mesh, in_specs=in_specs, out_specs=out_specs, check_vma=False)
        return run(seq_in, conv_norm, conv_weight, *rest)

    return step
```

```python
import functools
import itertools

import jax
import jax.numpy as jnp
from jax import lax
from jax.experimental import pallas as pl
from jax.experimental.pallas import tpu as pltpu
from jax.sharding import PartitionSpec as P

AXES = ("groups", "seq", "strand", "chan")
BF16, F32 = jnp.bfloat16, jnp.float32
PARAMS = pltpu.CompilerParams(vmem_limit_bytes=40 * 2**20)
VMEM_SPEC = pl.BlockSpec(memory_space=pltpu.VMEM)


def normalize(values, gain):
    return values * lax.rsqrt(jnp.mean(values * values, axis=-1, keepdims=True) + 1e-06) * gain


def matmul(left, right):
    return jnp.dot(left, right, preferred_element_type=F32)


def matmul_nt(left, right):
    return lax.dot_general(left, right, (((1,), (1,)), ((), ())), preferred_element_type=F32)


def passed_along(value, axis, steps):
    count = lax.axis_size(axis)
    initial, last = (max(0, -steps), min(count, count - steps))
    return lax.ppermute(value, axis, [(source, source + steps) for source in range(initial, last)])


def swapped(x, axis, stride):
    return lax.ppermute(x, axis, [(i, i ^ 1 << stride) for i in range(lax.axis_size(axis))])


def local_plain(
    seq_in, conv_norm, conv_weight, ff_norm, up_weight, down_weight,
    head_norm, value_weight, gate_weight, out_weight,
):
    state = seq_in[0].astype(F32)
    seq_count = lax.axis_size("seq")
    for block in range(conv_weight.shape[0]):
        reach = min(2**block, seq_count // 2)
        normed = normalize(state, conv_norm[block]).astype(BF16)
        before = passed_along(normed, "seq", reach)
        after = passed_along(normed, "seq", -reach)
        piece = lax.all_gather(conv_weight[block], ("seq", "chan"), axis=2, tiled=True)
        total = matmul(before, piece[0]) + matmul(normed, piece[1]) + matmul(after, piece[2])
        state = state + total.astype(BF16).astype(F32)
        mixed = normalize(state, ff_norm[block]).astype(BF16)
        up = lax.all_gather(up_weight[block], ("seq", "chan"), axis=1, tiled=True)
        hidden = jax.nn.gelu(matmul(mixed, up)).astype(BF16)
        down = lax.all_gather(down_weight[block], ("seq", "chan"), axis=0, tiled=True)
        state = state + matmul(hidden, down)
    final = normalize(state, head_norm).astype(BF16)
    value = matmul(final, value_weight)
    bit_count = (seq_count * lax.axis_size("chan")).bit_length() - 1
    opposite = swapped(final, "strand", 0)
    for digit in range(bit_count):
        opposite = swapped(opposite, ("seq", "chan"), digit)
    opposite = jnp.flip(opposite, 0)
    mirrored = matmul(opposite, gate_weight).astype(BF16)
    gated = (value * jax.nn.sigmoid(mirrored.astype(F32))).astype(BF16)
    return matmul(gated, out_weight).astype(BF16)[None]


def moved(value, go):
    sizes = [lax.axis_size(a) for a in AXES]

    def flat(at):
        number = 0
        for n, k in zip(sizes, at):
            number = number * n + k
        return number

    pairs = [(flat(at), flat(go(*at))) for at in itertools.product(*map(range, sizes))]
    return lax.ppermute(value, AXES, pairs)


def across(value):
    return moved(value, lambda g, i, s, c: (g, i, s, 1 - c))


def planes(value):
    return moved(value, lambda g, i, s, c: (1 - g, i, s, c))


def other_core(value):
    return moved(value, lambda g, i, s, c: (g, i, 1 - s, c))


def along(value):
    n = lax.axis_size("seq")
    return moved(value, lambda g, i, s, c: (g, (i + 1 - 2 * g) % n, s, c))


def after(values, events):
    values, _ = lax.optimization_barrier((tuple(values), tuple(events)))
    return values


def origins():
    g, i, c = (lax.axis_index(a) for a in ("groups", "seq", "chan"))
    n, m = lax.axis_size("seq"), lax.axis_size("chan")
    a = lax.rem(i + n - 1 + 2 * g, n)
    b = lax.rem(i + 2, n)
    ya = lax.rem(i + n + 1 - 2 * g, n)
    x = 1 - c
    at = [(i, c), (a, c), (b, c), (i, x), (a, x), (b, x), (ya, c), (ya, x)]
    return [k * m + h for k, h in at]


def pack_kernel(plan, mine, *refs):
    blocks, turned = plan
    refs, (out, wide, sems) = refs[:-3], refs[-3:]
    s = lax.axis_index("strand")
    part = s if mine else 1 - s
    at, turns, copies = 0, [], []

    def copy(source, target):
        copies.append(pltpu.make_async_copy(source, target, sems.at[len(copies)]))
        copies[-1].start()

    for ref, block, turn in zip(refs, blocks, turned):
        if turn:
            half = ref.shape[2] // 2
            columns = pl.ds(pl.multiple_of(part * half, half), half)
            copy(ref.at[block, :, columns], wide.at[len(turns)])
            turns.append((at, half, copies[-1]))
            at += half
        else:
            half = ref.shape[-2] // 2
            rows = pl.ds(pl.multiple_of(part * half, half), half)
            for tap in range(ref.shape[1]) if len(ref.shape) == 4 else (None,):
                source = ref.at[block, rows] if tap is None else ref.at[block, tap, rows]
                copy(source, out.at[at : at + half])
                at += half
    for k, (at, half, done) in enumerate(turns):
        done.wait()
        out[at : at + half] = wide[k].T
    for done in copies:
        if all(done is not turn[2] for turn in turns):
            done.wait()


def pack(arrays, blocks, turned, rows, mine):
    width = arrays[0].shape[1]
    half = arrays[0].shape[2] // 2
    return pl.pallas_call(
        functools.partial(pack_kernel, (blocks, turned), mine),
        out_shape=jax.ShapeDtypeStruct((rows, width), BF16),
        in_specs=[pl.BlockSpec(memory_space=pltpu.HBM)] * len(arrays),
        out_specs=VMEM_SPEC,
        scratch_shapes=[
            pltpu.VMEM((sum(turned), width, half), BF16),
            pltpu.SemaphoreType.DMA((2 * rows // 32,)),
        ],
        compiler_params=PARAMS,
        name="pack_own" if mine else "pack_rest",
    )(*[pltpu.with_memory_space_constraint(v, pltpu.HBM) for v in arrays])


def split_kernel(rows_ref, *out_refs):
    n = lax.axis_size("seq")
    i, s = lax.axis_index("seq"), lax.axis_index("strand")
    size = out_refs[0].shape[0]
    for k, out in enumerate(out_refs):
        j = i ^ k
        sub = jnp.where(s == 0, j, n - 1 - j)
        out[...] = rows_ref[pl.ds(pl.multiple_of(sub * size, size), size)]


def join_kernel(*refs):
    *parts, out = refs
    n = lax.axis_size("seq")
    i, s = lax.axis_index("seq"), lax.axis_index("strand")
    size = parts[0].shape[0]
    for k, part in enumerate(parts):
        j = i ^ k
        sub = jnp.where(s == 0, j, n - 1 - j)
        out[pl.ds(pl.multiple_of(sub * size, size), size)] = part[...]


def conv_kernel(block, parts, places, start, gain_ref, *refs):
    n = lax.axis_size("seq")
    states, arrays = refs[:parts], refs[parts:-3]
    out, weight, acc = refs[-3:]
    width = acc.shape[1]
    taps = weight.shape[0] // width
    half = width // len(places[0]) // 2
    s, j = lax.axis_index("strand"), lax.axis_index("seq")
    for side, part in zip(places, (s, 1 - s)):
        for (k, row), shard in zip(side, origins()):
            at = pl.multiple_of((shard * 2 + part) * half, half)
            for tap in range(taps):
                first = row + start + tap * half
                weight[pl.ds(tap * width + at, half)] = arrays[k][first : first + half]
    if parts > 1:
        size = states[0].shape[0]
        for k, state in enumerate(states):
            at = j ^ k
            out[pl.ds(pl.multiple_of(at * size, size), size)] = state[...].astype(F32)
        state = out[...]
    else:
        state = states[0][...]
    normed = normalize(state, gain_ref[block : block + 1]).astype(BF16)
    shift = state.shape[0] // n * min(2**block, n // 2)
    acc[...] = matmul_nt(normed, weight[width : 2 * width])
    acc[shift:] += matmul_nt(normed[:-shift], weight[:width])
    acc[:-shift] += matmul_nt(normed[shift:], weight[2 * width :])
    out[...] = state + acc[...].astype(BF16).astype(F32)


def conv(states, gain, arrays, places, block, start, taps):
    width = gain.shape[1]
    rows = sum(v.shape[0] for v in states)
    return pl.pallas_call(
        functools.partial(conv_kernel, block, len(states), places, start),
        out_shape=jax.ShapeDtypeStruct((rows, width), F32),
        in_specs=[VMEM_SPEC] * (1 + len(states) + len(arrays)),
        out_specs=VMEM_SPEC,
        scratch_shapes=[pltpu.VMEM((taps * width, width), BF16), pltpu.VMEM((rows, width), F32)],
        compiler_params=PARAMS,
        name=f"conv{block}",
    )(gain, *states, *arrays)


def ff_kernel(block, first, ends, places, start, half, gain_ref, head_ref, state_ref, *refs):
    if not first:
        mixed_ref, refs = refs[0], refs[1:]
    arrays, out, hid = refs, refs[-2 if ends else -3], refs[-1]
    state = state_ref[...]
    if first:
        mixed = normalize(state, gain_ref[block : block + 1]).astype(BF16)
    else:
        mixed = mixed_ref[...]
    down = []
    for r, pair in enumerate(zip(*places)):
        up = jnp.concatenate([arrays[k][row + start : row + start + half] for k, row in pair], 0)
        hid[:, 2 * r * half : 2 * (r + 1) * half] = jax.nn.gelu(matmul_nt(mixed, up)).astype(BF16)
        down += [arrays[k][row + start + half : row + start + 2 * half] for k, row in pair]
    state = state + matmul(hid[...], jnp.concatenate(down, 0))
    if ends == "head":
        state = normalize(state, head_ref[...]).astype(BF16)
    out[...] = state
    if not ends:
        refs[-2][...] = mixed


def feed_forward(state, mixed, gain, head, arrays, places, block, start, half, ends):
    rows, width = state.shape
    out = [jax.ShapeDtypeStruct((rows, width), BF16 if ends == "head" else F32)]
    if not ends:
        out.append(jax.ShapeDtypeStruct((rows, width), BF16))
    given = [state] if mixed is None else [state, mixed]
    return pl.pallas_call(
        functools.partial(ff_kernel, block, mixed is None, ends, places, start, half),
        out_shape=out,
        in_specs=[VMEM_SPEC] * (2 + len(given) + len(arrays)),
        out_specs=[VMEM_SPEC] * len(out),
        scratch_shapes=[pltpu.VMEM((rows, 2 * len(places[0]) * half), BF16)],
        compiler_params=PARAMS,
        name=f"ff{block}",
    )(gain, head, *given, *arrays)


def head_kernel(sends, final_ref, opposite_ref, value_ref, gate_ref, out_ref, *refs):
    *outs, result = refs
    n = len(outs)
    size = outs[0].shape[0]
    j = lax.axis_index("seq")
    value = matmul(final_ref[...], value_ref[...])
    row = lax.broadcasted_iota(jnp.int32, (size, size), 0)
    col = lax.broadcasted_iota(jnp.int32, (size, size), 1)
    reverse = jnp.where(row + col == size - 1, 1.0, 0.0).astype(BF16)
    flipped = [
        matmul(reverse, opposite_ref[(n - 1 - i) * size : (n - i) * size]).astype(BF16) for i in range(n)
    ]
    mirrored = matmul(jnp.concatenate(flipped, 0), gate_ref[...]).astype(BF16)
    gated = (value * jax.nn.sigmoid(mirrored.astype(F32))).astype(BF16)
    result[...] = matmul(gated, out_ref[...]).astype(BF16)
    for k, out in zip(sends, outs):
        at = j ^ k
        out[...] = result[pl.ds(pl.multiple_of(at * size, size), size)]


def local_spread(
    seq_in, conv_norm, conv_weight, ff_norm, up_weight, down_weight,
    head_norm, value_weight, gate_weight, out_weight,
):
    n = lax.axis_size("seq")
    blocks, taps, width, chans = conv_weight.shape
    hidden = up_weight.shape[2]
    half = hidden // 2
    rows = seq_in.shape[1]
    part = jax.ShapeDtypeStruct((rows // n, width), BF16)
    turned = jnp.swapaxes(conv_weight, 2, 3)
    cut = hidden + taps * chans
    shard = (up_weight, down_weight, turned, turned, up_weight, down_weight)
    which = (0, 0, 0, 1, 1, 1), (True, False, False, False, True, False)
    own = pack(shard, *which, cut + hidden, True)
    to = lambda k: (lambda g, i, s, c: (g, i ^ k, s, c if s == 0 else 1 - c))
    parts = pl.pallas_call(
        split_kernel, out_shape=[part] * n, in_specs=[VMEM_SPEC], out_specs=[VMEM_SPEC] * n,
        compiler_params=PARAMS, name="split",
    )(seq_in[0])

    a = along(own)
    x = across(own)
    b = along(a)
    xa = across(a)
    ya = planes(a)
    swaps = [other_core(a), other_core(x)]
    states = [moved(parts[0], to(0))]
    first = after(shard[:3], [x])
    rest = pack((*first[:3], first[2], *first[:2]), *which, cut + hidden, False)
    b, xa, ya, rest, swaps[0], swaps[1], states[0], *parts = after(
        [b, xa, ya, rest, *swaps, states[0], *parts[1:]], []
    )
    yxa0 = planes(xa[:cut])
    xb0 = across(b[:cut])
    states += [moved(p, to(k + 1)) for k, p in enumerate(parts)]
    bl, xal, yal, xb0, yxa0, *states = after([b, xa, ya, xb0, yxa0, *states], [])
    stay = [bl, xal, yal]
    swap0 = other_core(jnp.concatenate([*(v[:cut] for v in stay), xb0, yxa0], 0))
    yxa1 = planes(xal[cut:])
    xb1 = across(bl[cut:])
    mine = [own, a, b, x, xa, ya]
    others = [rest, *swaps]
    arrays = mine + [xb0, yxa0] + others + [swap0]
    places = [
        [(k, 0) for k in (0, 1, 2, 3, 4, 6, 5, 7)],
        [(8, 0), (9, 0), (11, 0), (10, 0), (11, cut), (11, 3 * cut), (11, 2 * cut), (11, 4 * cut)],
    ]
    early = [
        [(k, cut) for k in range(6)],
        [(6, cut), (7, cut), (9, 0), (8, cut), (9, hidden), (9, 2 * hidden)],
    ]
    head = head_norm[None]
    state = conv0 = conv(states, conv_norm, arrays, places, 0, hidden, taps)
    (state,) = (ff0,) = feed_forward(state, None, ff_norm, head, arrays, places, 0, 0, half, "state")
    state = conv1 = conv([state], conv_norm, arrays, places, 1, hidden + taps * chans // 2, taps)
    tail, _ = lax.optimization_barrier((jnp.concatenate([v[cut:] for v in stay], 0), conv0))
    swap1 = other_core(tail)
    state, mixed = feed_forward(
        state, None, ff_norm, head, mine + others + [swap1], early, 1, 0, half, ""
    )
    late = jnp.concatenate(after([xb1, yxa1], [conv1]), 0)
    places = [[(0, 0), (0, hidden)], [(1, 0), (1, hidden)]]
    arrays = [late, other_core(late)]
    (final,) = feed_forward(state, mixed, ff_norm, head, arrays, places, 1, 0, half, "head")
    opposite = other_core(final)
    sends = [2, 3, 1, 0]
    results = pl.pallas_call(
        functools.partial(head_kernel, sends), out_shape=[part] * n, in_specs=[VMEM_SPEC] * 5, out_specs=[VMEM_SPEC] * n,
        scratch_shapes=[pltpu.VMEM((rows, width), BF16)], compiler_params=PARAMS, name="head",
    )(final, opposite, value_weight, gate_weight, out_weight)
    ready = dict(zip(sends, results))
    home = {k: moved(ready[k], to(k)) for k in sends if k}
    (near,) = after([ready[0]], [home[1]])
    home = [moved(near, to(0))] + [home[k] for k in range(1, n)]
    joined = pl.pallas_call(
        join_kernel, out_shape=jax.ShapeDtypeStruct((rows, width), BF16), in_specs=[VMEM_SPEC] * n,
        out_specs=VMEM_SPEC, compiler_params=PARAMS, name="join",
    )(*home)
    return joined[None]


def solution(mesh):
    in_specs = (
        P("strand", ("groups", "seq", "chan"), None),
        P(),
        P(None, None, None, ("seq", "chan")),
        P(),
        P(None, None, ("seq", "chan")),
        P(None, ("seq", "chan"), None),
        P(),
        P(),
        P(),
        P(),
    )
    out_specs = P("strand", ("groups", "seq", "chan"), None)

    def step(seq_in, conv_norm, conv_weight, *rest):
        size = mesh.shape
        shards = size["seq"] * size["chan"]
        tiled = conv_weight.shape[3] % (32 * shards) == 0
        blocks = conv_weight.shape[0]
        spread = tiled and blocks == 2 and [size[a] for a in AXES] == [2, 4, 2, 2]
        local = local_spread if spread else local_plain
        run = jax.shard_map(local, mesh=mesh, in_specs=in_specs, out_specs=out_specs, check_vma=False)
        return run(seq_in, conv_norm, conv_weight, *rest)

    return step
```

```python
import functools
import itertools

import jax
import jax.numpy as jnp
from jax import lax
from jax.experimental import pallas as pl
from jax.experimental.pallas import tpu as pltpu
from jax.sharding import PartitionSpec as P

AXES = ("groups", "seq", "strand", "chan")
BF16, F32 = jnp.bfloat16, jnp.float32
PARAMS = pltpu.CompilerParams(vmem_limit_bytes=40 * 2**20)
VMEM_SPEC = pl.BlockSpec(memory_space=pltpu.VMEM)


def normalize(values, gain):
    return values * lax.rsqrt(jnp.mean(values * values, axis=-1, keepdims=True) + 1e-06) * gain


def matmul(left, right):
    return jnp.dot(left, right, preferred_element_type=F32)


def matmul_nt(left, right):
    return lax.dot_general(left, right, (((1,), (1,)), ((), ())), preferred_element_type=F32)


def passed_along(value, axis, steps):
    count = lax.axis_size(axis)
    initial, last = (max(0, -steps), min(count, count - steps))
    return lax.ppermute(value, axis, [(source, source + steps) for source in range(initial, last)])


def swapped(x, axis, stride):
    return lax.ppermute(x, axis, [(i, i ^ 1 << stride) for i in range(lax.axis_size(axis))])


def local_plain(
    seq_in, conv_norm, conv_weight, ff_norm, up_weight, down_weight,
    head_norm, value_weight, gate_weight, out_weight,
):
    state = seq_in[0].astype(F32)
    seq_count = lax.axis_size("seq")
    for block in range(conv_weight.shape[0]):
        reach = min(2**block, seq_count // 2)
        normed = normalize(state, conv_norm[block]).astype(BF16)
        before = passed_along(normed, "seq", reach)
        after = passed_along(normed, "seq", -reach)
        piece = lax.all_gather(conv_weight[block], ("seq", "chan"), axis=2, tiled=True)
        total = matmul(before, piece[0]) + matmul(normed, piece[1]) + matmul(after, piece[2])
        state = state + total.astype(BF16).astype(F32)
        mixed = normalize(state, ff_norm[block]).astype(BF16)
        up = lax.all_gather(up_weight[block], ("seq", "chan"), axis=1, tiled=True)
        hidden = jax.nn.gelu(matmul(mixed, up)).astype(BF16)
        down = lax.all_gather(down_weight[block], ("seq", "chan"), axis=0, tiled=True)
        state = state + matmul(hidden, down)
    final = normalize(state, head_norm).astype(BF16)
    value = matmul(final, value_weight)
    bit_count = (seq_count * lax.axis_size("chan")).bit_length() - 1
    opposite = swapped(final, "strand", 0)
    for digit in range(bit_count):
        opposite = swapped(opposite, ("seq", "chan"), digit)
    opposite = jnp.flip(opposite, 0)
    mirrored = matmul(opposite, gate_weight).astype(BF16)
    gated = (value * jax.nn.sigmoid(mirrored.astype(F32))).astype(BF16)
    return matmul(gated, out_weight).astype(BF16)[None]


def moved(value, go):
    sizes = [lax.axis_size(a) for a in AXES]

    def flat(at):
        number = 0
        for n, k in zip(sizes, at):
            number = number * n + k
        return number

    pairs = [(flat(at), flat(go(*at))) for at in itertools.product(*map(range, sizes))]
    return lax.ppermute(value, AXES, pairs)


def across(value):
    return moved(value, lambda g, i, s, c: (g, i, s, 1 - c))


def planes(value):
    return moved(value, lambda g, i, s, c: (1 - g, i, s, c))


def other_core(value):
    return moved(value, lambda g, i, s, c: (g, i, 1 - s, c))


def along(value):
    n = lax.axis_size("seq")
    return moved(value, lambda g, i, s, c: (g, (i + 1 - 2 * g) % n, s, c))


def after(values, events):
    values, _ = lax.optimization_barrier((tuple(values), tuple(events)))
    return values


def origins():
    g, i, c = (lax.axis_index(a) for a in ("groups", "seq", "chan"))
    n, m = lax.axis_size("seq"), lax.axis_size("chan")
    a = lax.rem(i + n - 1 + 2 * g, n)
    b = lax.rem(i + 2, n)
    ya = lax.rem(i + n + 1 - 2 * g, n)
    x = 1 - c
    at = [(i, c), (a, c), (b, c), (i, x), (a, x), (b, x), (ya, c), (ya, x)]
    return [k * m + h for k, h in at]


def pack_kernel(plan, mine, *refs):
    blocks, turned = plan
    refs, (out, wide, sems) = refs[:-3], refs[-3:]
    s = lax.axis_index("strand")
    part = s if mine else 1 - s
    at, turns, copies = 0, [], []

    def copy(source, target):
        copies.append(pltpu.make_async_copy(source, target, sems.at[len(copies)]))
        copies[-1].start()

    for ref, block, turn in zip(refs, blocks, turned):
        if turn:
            half = ref.shape[2] // 2
            columns = pl.ds(pl.multiple_of(part * half, half), half)
            copy(ref.at[block, :, columns], wide.at[len(turns)])
            turns.append((at, half, copies[-1]))
            at += half
        else:
            half = ref.shape[-2] // 2
            rows = pl.ds(pl.multiple_of(part * half, half), half)
            for tap in range(ref.shape[1]) if len(ref.shape) == 4 else (None,):
                source = ref.at[block, rows] if tap is None else ref.at[block, tap, rows]
                copy(source, out.at[at : at + half])
                at += half
    for k, (at, half, done) in enumerate(turns):
        done.wait()
        out[at : at + half] = wide[k].T
    for done in copies:
        if all(done is not turn[2] for turn in turns):
            done.wait()


def pack(arrays, blocks, turned, rows, mine):
    width = arrays[0].shape[1]
    half = arrays[0].shape[2] // 2
    return pl.pallas_call(
        functools.partial(pack_kernel, (blocks, turned), mine),
        out_shape=jax.ShapeDtypeStruct((rows, width), BF16),
        in_specs=[pl.BlockSpec(memory_space=pltpu.HBM)] * len(arrays),
        out_specs=VMEM_SPEC,
        scratch_shapes=[
            pltpu.VMEM((sum(turned), width, half), BF16),
            pltpu.SemaphoreType.DMA((2 * rows // 32,)),
        ],
        compiler_params=PARAMS,
        name="pack_own" if mine else "pack_rest",
    )(*[pltpu.with_memory_space_constraint(v, pltpu.HBM) for v in arrays])


def split_kernel(rows_ref, *out_refs):
    n = lax.axis_size("seq")
    i, s = lax.axis_index("seq"), lax.axis_index("strand")
    size = out_refs[0].shape[0]
    for k, out in enumerate(out_refs):
        j = i ^ k
        sub = jnp.where(s == 0, j, n - 1 - j)
        out[...] = rows_ref[pl.ds(pl.multiple_of(sub * size, size), size)]


def join_kernel(order, *refs):
    parts, out, sems = refs[: len(order)], refs[-2], refs[-1]
    n = lax.axis_size("seq")
    i, s = lax.axis_index("seq"), lax.axis_index("strand")
    size = parts[0].shape[0]
    copies = []
    for k, part in zip(order, parts):
        j = i ^ k
        sub = jnp.where(s == 0, j, n - 1 - j)
        rows = pl.ds(pl.multiple_of(sub * size, size), size)
        copies.append(pltpu.make_async_copy(part, out.at[rows], sems.at[len(copies)]))
        copies[-1].start()
    for copy in copies:
        copy.wait()


def join(parts, order, begun, shape):
    hbm = pl.BlockSpec(memory_space=pltpu.HBM)
    extra = [] if begun is None else [begun]
    return pl.pallas_call(
        functools.partial(join_kernel, order),
        out_shape=shape,
        in_specs=[VMEM_SPEC] * len(parts) + [hbm] * len(extra),
        out_specs=hbm,
        scratch_shapes=[pltpu.SemaphoreType.DMA((len(parts),))],
        input_output_aliases={len(parts): 0} if extra else {},
        compiler_params=PARAMS,
        name="join_rest" if extra else "join_first",
    )(*parts, *extra)


def conv_kernel(block, parts, places, start, gain_ref, *refs):
    n = lax.axis_size("seq")
    states, arrays = refs[:parts], refs[parts:-3]
    out, weight, acc = refs[-3:]
    width = acc.shape[1]
    taps = weight.shape[0] // width
    half = width // len(places[0]) // 2
    s, j = lax.axis_index("strand"), lax.axis_index("seq")
    for side, part in zip(places, (s, 1 - s)):
        for (k, row), shard in zip(side, origins()):
            at = pl.multiple_of((shard * 2 + part) * half, half)
            for tap in range(taps):
                first = row + start + tap * half
                weight[pl.ds(tap * width + at, half)] = arrays[k][first : first + half]
    if parts > 1:
        size = states[0].shape[0]
        for k, state in enumerate(states):
            at = j ^ k
            out[pl.ds(pl.multiple_of(at * size, size), size)] = state[...].astype(F32)
        state = out[...]
    else:
        state = states[0][...]
    normed = normalize(state, gain_ref[block : block + 1]).astype(BF16)
    shift = state.shape[0] // n * min(2**block, n // 2)
    acc[...] = matmul_nt(normed, weight[width : 2 * width])
    acc[shift:] += matmul_nt(normed[:-shift], weight[:width])
    acc[:-shift] += matmul_nt(normed[shift:], weight[2 * width :])
    out[...] = state + acc[...].astype(BF16).astype(F32)


def conv(states, gain, arrays, places, block, start, taps):
    width = gain.shape[1]
    rows = sum(v.shape[0] for v in states)
    return pl.pallas_call(
        functools.partial(conv_kernel, block, len(states), places, start),
        out_shape=jax.ShapeDtypeStruct((rows, width), F32),
        in_specs=[VMEM_SPEC] * (1 + len(states) + len(arrays)),
        out_specs=VMEM_SPEC,
        scratch_shapes=[pltpu.VMEM((taps * width, width), BF16), pltpu.VMEM((rows, width), F32)],
        compiler_params=PARAMS,
        name=f"conv{block}",
    )(gain, *states, *arrays)


def ff_kernel(block, first, ends, places, start, half, gain_ref, head_ref, state_ref, *refs):
    if not first:
        mixed_ref, refs = refs[0], refs[1:]
    arrays, out, hid = refs, refs[-2 if ends else -3], refs[-1]
    state = state_ref[...]
    if first:
        mixed = normalize(state, gain_ref[block : block + 1]).astype(BF16)
    else:
        mixed = mixed_ref[...]
    down = []
    for r, pair in enumerate(zip(*places)):
        up = jnp.concatenate([arrays[k][row + start : row + start + half] for k, row in pair], 0)
        hid[:, 2 * r * half : 2 * (r + 1) * half] = jax.nn.gelu(matmul_nt(mixed, up)).astype(BF16)
        down += [arrays[k][row + start + half : row + start + 2 * half] for k, row in pair]
    state = state + matmul(hid[...], jnp.concatenate(down, 0))
    if ends == "head":
        state = normalize(state, head_ref[...]).astype(BF16)
    out[...] = state
    if not ends:
        refs[-2][...] = mixed


def feed_forward(state, mixed, gain, head, arrays, places, block, start, half, ends):
    rows, width = state.shape
    out = [jax.ShapeDtypeStruct((rows, width), BF16 if ends == "head" else F32)]
    if not ends:
        out.append(jax.ShapeDtypeStruct((rows, width), BF16))
    given = [state] if mixed is None else [state, mixed]
    return pl.pallas_call(
        functools.partial(ff_kernel, block, mixed is None, ends, places, start, half),
        out_shape=out,
        in_specs=[VMEM_SPEC] * (2 + len(given) + len(arrays)),
        out_specs=[VMEM_SPEC] * len(out),
        scratch_shapes=[pltpu.VMEM((rows, 2 * len(places[0]) * half), BF16)],
        compiler_params=PARAMS,
        name=f"ff{block}",
    )(gain, head, *given, *arrays)


def value_kernel(final_ref, weight_ref, value_ref):
    value_ref[...] = matmul(final_ref[...], weight_ref[...])


def head_kernel(sends, value_ref, opposite_ref, gate_ref, out_ref, *refs):
    *outs, result = refs
    n = len(outs)
    size = outs[0].shape[0]
    j = lax.axis_index("seq")
    value = value_ref[...]
    row = lax.broadcasted_iota(jnp.int32, (size, size), 0)
    col = lax.broadcasted_iota(jnp.int32, (size, size), 1)
    reverse = jnp.where(row + col == size - 1, 1.0, 0.0).astype(BF16)
    flipped = [
        matmul(reverse, opposite_ref[(n - 1 - i) * size : (n - i) * size]).astype(BF16) for i in range(n)
    ]
    mirrored = matmul(jnp.concatenate(flipped, 0), gate_ref[...]).astype(BF16)
    gated = (value * jax.nn.sigmoid(mirrored.astype(F32))).astype(BF16)
    result[...] = matmul(gated, out_ref[...]).astype(BF16)
    for k, out in zip(sends, outs):
        at = j ^ k
        out[...] = result[pl.ds(pl.multiple_of(at * size, size), size)]


def local_spread(
    seq_in, conv_norm, conv_weight, ff_norm, up_weight, down_weight,
    head_norm, value_weight, gate_weight, out_weight,
):
    n = lax.axis_size("seq")
    blocks, taps, width, chans = conv_weight.shape
    hidden = up_weight.shape[2]
    half = hidden // 2
    rows = seq_in.shape[1]
    part = jax.ShapeDtypeStruct((rows // n, width), BF16)
    turned = jnp.swapaxes(conv_weight, 2, 3)
    cut = hidden + taps * chans
    shard = (up_weight, down_weight, turned, turned, up_weight, down_weight)
    which = (0, 0, 0, 1, 1, 1), (True, False, False, False, True, False)
    own = pack(shard, *which, cut + hidden, True)
    to = lambda k: (lambda g, i, s, c: (g, i ^ k, s, c if s == 0 else 1 - c))
    parts = pl.pallas_call(
        split_kernel, out_shape=[part] * n, in_specs=[VMEM_SPEC], out_specs=[VMEM_SPEC] * n,
        compiler_params=PARAMS, name="split",
    )(seq_in[0])

    a = along(own)
    x = across(own)
    a, x = after([a, x], [])
    b = along(a)
    xa = across(a)
    ya = planes(a)
    swaps = [other_core(a), other_core(x)]
    states = [moved(parts[0], to(0))]
    first = after(shard[:3], [x])
    rest = pack((*first[:3], first[2], *first[:2]), *which, cut + hidden, False)
    b, xa, ya, rest, swaps[0], swaps[1], states[0], *parts = after(
        [b, xa, ya, rest, *swaps, states[0], *parts[1:]], []
    )
    yxa0 = planes(xa[:cut])
    xb0 = across(b[:cut])
    states += [moved(p, to(k + 1)) for k, p in enumerate(parts)]
    bl, xal, yal, xb0, yxa0, *states = after([b, xa, ya, xb0, yxa0, *states], [])
    stay = [bl, xal, yal]
    swap0 = other_core(jnp.concatenate([*(v[:cut] for v in stay), xb0, yxa0], 0))
    yxa1 = planes(xal[cut:])
    xb1 = across(bl[cut:])
    mine = [own, a, b, x, xa, ya]
    others = [rest, *swaps]
    arrays = mine + [xb0, yxa0] + others + [swap0]
    places = [
        [(k, 0) for k in (0, 1, 2, 3, 4, 6, 5, 7)],
        [(8, 0), (9, 0), (11, 0), (10, 0), (11, cut), (11, 3 * cut), (11, 2 * cut), (11, 4 * cut)],
    ]
    early = [
        [(k, cut) for k in range(6)],
        [(6, cut), (7, cut), (9, 0), (8, cut), (9, hidden), (9, 2 * hidden)],
    ]
    head = head_norm[None]
    state = conv0 = conv(states, conv_norm, arrays, places, 0, hidden, taps)
    (state,) = (ff0,) = feed_forward(state, None, ff_norm, head, arrays, places, 0, 0, half, "state")
    state = conv1 = conv([state], conv_norm, arrays, places, 1, hidden + taps * chans // 2, taps)
    tail, _ = lax.optimization_barrier((jnp.concatenate([v[cut:] for v in stay], 0), conv0))
    swap1 = other_core(tail)
    state, mixed = feed_forward(
        state, None, ff_norm, head, mine + others + [swap1], early, 1, 0, half, ""
    )
    late = jnp.concatenate(after([xb1, yxa1], [conv1]), 0)
    places = [[(0, 0), (0, hidden)], [(1, 0), (1, hidden)]]
    arrays = [late, other_core(late)]
    (final,) = feed_forward(state, mixed, ff_norm, head, arrays, places, 1, 0, half, "head")
    opposite = other_core(final)
    value = pl.pallas_call(
        value_kernel, out_shape=jax.ShapeDtypeStruct((rows, width), F32), in_specs=[VMEM_SPEC] * 2,
        out_specs=VMEM_SPEC, compiler_params=PARAMS, name="value",
    )(final, value_weight)
    sends = [2, 3, 1, 0]
    results = pl.pallas_call(
        functools.partial(head_kernel, sends), out_shape=[part] * n, in_specs=[VMEM_SPEC] * 4, out_specs=[VMEM_SPEC] * n,
        scratch_shapes=[pltpu.VMEM((rows, width), BF16)], compiler_params=PARAMS, name="head",
    )(value, opposite, gate_weight, out_weight)
    ready = dict(zip(sends, results))
    home = {k: moved(ready[k], to(k)) for k in sends if k}
    (near,) = after([ready[0]], [home[1]])
    home = [moved(near, to(0))] + [home[k] for k in range(1, n)]
    whole = jax.ShapeDtypeStruct((rows, width), BF16)
    joined = None
    for order in ((1,), (0, 2, 3)):
        joined = join([home[k] for k in order], order, joined, whole)
    return joined[None]


def solution(mesh):
    in_specs = (
        P("strand", ("groups", "seq", "chan"), None),
        P(),
        P(None, None, None, ("seq", "chan")),
        P(),
        P(None, None, ("seq", "chan")),
        P(None, ("seq", "chan"), None),
        P(),
        P(),
        P(),
        P(),
    )
    out_specs = P("strand", ("groups", "seq", "chan"), None)

    def step(seq_in, conv_norm, conv_weight, *rest):
        size = mesh.shape
        shards = size["seq"] * size["chan"]
        tiled = conv_weight.shape[3] % (32 * shards) == 0
        blocks = conv_weight.shape[0]
        spread = tiled and blocks == 2 and [size[a] for a in AXES] == [2, 4, 2, 2]
        local = local_spread if spread else local_plain
        run = jax.shard_map(local, mesh=mesh, in_specs=in_specs, out_specs=out_specs, check_vma=False)
        return run(seq_in, conv_norm, conv_weight, *rest)

    return step
```
